32 devices in a mesh: rows: 4 (over y, core), seq: 8 (over z, x).
Axes of the slice: x: 2, y: 2, z: 4, core: 2. Of those that a mesh axis runs over, the one named last changes fastest.
Arguments:
- tokens: bfloat16 [4, 4096, 640], P('rows', 'seq'), may hold values from -6 to 6
- segments: int32 [4, 4096], P('rows', 'seq'), may hold values from 0 to 7, never falling along the last dimension, each value on 1 to 1024 neighbouring positions
- ln1_gain: bfloat16 [640], replicated, may hold values from 0.25 to 1.75
- ln1_bias: bfloat16 [640], replicated, may hold values from -1.25 to 1.25
- w_qkv: bfloat16 [640, 1920], P('rows', 'seq'), may hold values from -0.25 to 0.25
- q_bias: bfloat16 [640], replicated, may hold values from -3 to 3
- v_bias: bfloat16 [640], replicated, may hold values from -0.3125 to 0.3125
- w_out: bfloat16 [640, 640], P('rows', 'seq'), may hold values from -2 to 2
- out_bias: bfloat16 [640], replicated, may hold values from -1.25 to 1.25
- ln2_gain: bfloat16 [640], replicated, may hold values from 0.25 to 1.75
- ln2_bias: bfloat16 [640], replicated, may hold values from -1.25 to 1.25
- w_up: bfloat16 [640, 5120], P('rows', 'seq'), may hold values from -0.25 to 0.25
- up_bias: bfloat16 [5120], replicated, may hold values from -1.75 to 1.75
- w_down: bfloat16 [5120, 640], P('seq', 'rows'), may hold values from -0.078125 to 0.078125
- down_bias: bfloat16 [640], replicated, may hold values from -1.25 to 1.25
- cotangent: bfloat16 [4, 4096, 640], P('rows', 'seq'), may hold values from -8 to 8
Outputs:
- output: bfloat16 [4, 4096, 640], P('rows', 'seq')
- tokens_grad: bfloat16 [4, 4096, 640], P('rows', 'seq')
- ln1_gain_grad: float32 [640], replicated
- ln1_bias_grad: float32 [640], replicated
- w_qkv_grad: float32 [640, 1920], P('rows', 'seq')
- q_bias_grad: float32 [640], replicated
- v_bias_grad: float32 [640], replicated
- w_out_grad: float32 [640, 640], P('rows', 'seq')
- out_bias_grad: float32 [640], replicated
- ln2_gain_grad: float32 [640], replicated
- ln2_bias_grad: float32 [640], replicated
- w_up_grad: float32 [640, 5120], P('rows', 'seq')
- up_bias_grad: float32 [5120], replicated
- w_down_grad: float32 [5120, 640], P('seq', 'rows')
- down_bias_grad: float32 [640], replicated
The draws below stay inside these ranges and needn't reach their ends.
Inputs may be any that keep to these rules, and one draw needn't show every extreme that they name: `segments`: ids never fall along a row; each segment holds 1 to 1024 positions.
All inputs are finite; a program needn't handle non-finite values.
Results may differ from the reference program's by a relative error of at most 0.015.
Values may be sent and summed in bfloat16 or wider, within the bound.
A program may use at most 128 MiB of HBM per device.

```python
import math
import jax
import jax.numpy as jnp
import numpy as np
from jax import lax

D = 640
HEADS = 20
HEAD = 32
FF = 5120
ROW_LEN = 4096
SEGS = 8
SEG_MOST = 1024
ROWS = 4


def strengthened(array, rng, source, target, blocks, factor):
    owner, partner = [(jnp.arange(array.shape[dim]) // (array.shape[dim] // blocks)).reshape([-1 if axis == dim else 1 for axis in range(array.ndim)]) for dim in (source, target)]
    chosen = jax.random.permutation(rng, blocks)[partner]
    strong = (owner == chosen) | (owner == (partner + blocks // 2) % blocks)
    return jnp.where(strong, factor * array, array)


def levels(stream_key, shape, pieces, smallest, high):
    loudness, own = 1.0, jax.random.fold_in(stream_key, 6)
    for axis_at, shards_of in pieces:
        heights = jnp.exp(jax.random.uniform(jax.random.fold_in(own, axis_at), (shards_of,), jnp.float32, smallest / len(pieces), high / len(pieces)))
        loudness = loudness * jnp.repeat(heights, shape[axis_at] // shards_of).reshape([-1 if axis == axis_at else 1 for axis in range(len(shape))])
    return loudness


def length_profile(number_of, total, bound, slope):
    loads = [(1 << 20) // math.isqrt(grade ** slope) + 1 for grade in range(2, number_of + 1)]
    spare, counts = total - bound - (number_of - 1), [1] * (number_of - 1)
    while spare > 0:
        free = [i for i in range(number_of - 1) if counts[i] < bound]
        whole, remaining = sum([loads[i] for i in free]), spare
        for i in free:
            extra = min(bound - counts[i], max(1, remaining * loads[i] // whole), spare)
            counts[i] = counts[i] + extra
            spare = spare - extra
    return np.array([bound] + counts)


def ragged(rng, count, total, limit, slope):
    if count == 2:
        one = jax.random.randint(rng, (), max(1, total - limit), min(limit, total - 1) + 1)
        return jnp.stack([one, total - one])
    tallies = jnp.asarray(length_profile(count, total, limit, slope), jnp.int32)
    couples = (count - 1) // 2
    donor, receiver = tallies[1:1 + 2 * couples:2], tallies[2:2 + 2 * couples:2]
    slack = jnp.minimum(donor - 1, limit - receiver)
    shifted = jax.random.randint(jax.random.fold_in(rng, 1), (couples,), 0, 1 << 20) % (slack + 1)
    tallies = tallies.at[1:1 + 2 * couples:2].set(donor - shifted).at[2:2 + 2 * couples:2].set(receiver + shifted)
    return tallies[jax.random.permutation(jax.random.fold_in(rng, 2), count)]


def gaussian(rng, shape, scale, most, shards=(), kind=jnp.bfloat16):
    values = scale * jax.random.normal(rng, shape, jnp.float32)
    if shards:
        values = values * levels(rng, shape, shards, -0.22, 0.18)
    return jnp.clip(values, -most, most).astype(kind)


def gaussian_with(stream_key, extent, deviation, limit, split, heavy, kind=jnp.bfloat16):
    drawn = deviation * jax.random.normal(stream_key, extent, jnp.float32)
    if split:
        drawn = drawn * levels(stream_key, extent, split, -0.22, 0.18)
    return jnp.clip(strengthened(drawn, jax.random.fold_in(stream_key, 3), *heavy), -limit, limit).astype(kind)


def setup_inputs(seed: int = 0) -> dict:
    key_of = jax.random.split(jax.random.key(seed), 17)
    return {
        "tokens": gaussian(key_of[0], (ROWS, ROW_LEN, D), 1.0, 6.0, ((0, 4), (1, 8))),
        "segments": jax.vmap(lambda own: jnp.searchsorted(jnp.cumsum(ragged(own, SEGS, ROW_LEN, SEG_MOST, 0)), jnp.arange(ROW_LEN), side="right"))(jax.random.split(key_of[1], ROWS)).reshape((ROWS, ROW_LEN)).astype(jnp.int32),
        "ln1_gain": jnp.clip(1.0 + 0.15 * jax.random.normal(key_of[2], (D,), jnp.float32), 0.25, 1.75).astype(jnp.bfloat16),
        "ln1_bias": gaussian(key_of[3], (D,), 0.2, 1.25),
        "w_qkv": gaussian(key_of[4], (D, 3 * D), D ** -0.5, 0.25, ((0, 4), (1, 8))),
        "q_bias": gaussian(key_of[5], (D,), 0.5, 3.0),
        "v_bias": gaussian(key_of[6], (D,), 0.05, 0.3125),
        "w_out": gaussian(key_of[7], (D, D), (max(1, D // 64)) ** -0.5, 2.0, ((0, 4), (1, 8))),
        "out_bias": gaussian(key_of[8], (D,), 0.2, 1.25),
        "ln2_gain": jnp.clip(1.0 + 0.15 * jax.random.normal(key_of[9], (D,), jnp.float32), 0.25, 1.75).astype(jnp.bfloat16),
        "ln2_bias": gaussian(key_of[10], (D,), 0.2, 1.25),
        "w_up": gaussian(key_of[11], (D, FF), D ** -0.5, 0.25, ((0, 4), (1, 8))),
        "up_bias": gaussian(key_of[12], (FF,), 0.3, 1.75),
        "w_down": gaussian(key_of[13], (FF, D), FF ** -0.5, 0.078125, ((0, 8), (1, 4))),
        "down_bias": gaussian(key_of[14], (D,), 0.2, 1.25),
        "cotangent": gaussian_with(key_of[15], (ROWS, ROW_LEN, D), 1.0, 8.0, ((0, 4), (1, 8)), (1, 2, 8, 2.0)),
    }


@jax.custom_vjp
def low(v):
    return lax.optimization_barrier(v.astype(jnp.bfloat16)).astype(jnp.float32)

@jax.custom_vjp
def low_back(v):
    return v

def low_keep(v):
    return (low(v), None)

def low_pass(kept, grad):
    return (grad,)

def back_keep(v):
    return (v, None)

def back_low(kept, grad):
    return (low(grad),)
low.defvjp(low_keep, low_pass)
low_back.defvjp(back_keep, back_low)
NORM_EPS = 1e-05
MASKED = -1000000000.0
HIGHEST = lax.Precision.HIGHEST

def layer_norm(value, gain, shift):
    centre = lax.optimization_barrier(jnp.mean(value, axis=-1, keepdims=True))
    centred = value - centre
    spread = lax.optimization_barrier(jnp.mean(centred * centred, axis=-1, keepdims=True))
    return centred * lax.rsqrt(spread + NORM_EPS) * gain + shift

def head_attention(queries, key_rows, value_rows, segment):
    scores = low_back(jnp.dot(queries, key_rows.T, precision=HIGHEST) * (1.0 / math.sqrt(HEAD)))
    same_doc = segment[:, None] == segment[None, :]
    scores = jnp.where(same_doc, scores, MASKED)
    row_max = lax.optimization_barrier(jnp.max(scores, axis=-1, keepdims=True))
    weights = jnp.exp(scores - row_max)
    prob_rows = weights / lax.optimization_barrier(jnp.sum(weights, axis=-1, keepdims=True))
    return jnp.dot(low(prob_rows), value_rows, precision=HIGHEST)

def row_forward(tokens_row, segment_row, ln1_gain, ln1_bias, w_qkv, q_bias, v_bias, w_out, out_bias, ln2_gain, ln2_bias, w_up, up_bias, w_down, down_bias):
    normed = low(layer_norm(tokens_row, ln1_gain, ln1_bias))
    qkv_bias = jnp.concatenate([q_bias, jnp.zeros_like(q_bias), v_bias])
    mixed = jnp.dot(normed, w_qkv, precision=HIGHEST) + qkv_bias
    mixed = low_back(low(mixed))
    per_head = mixed.reshape(ROW_LEN, 3, HEADS, HEAD).transpose(2, 1, 0, 3)
    checked = jax.checkpoint(head_attention)
    attended = lax.map(lambda head_parts: checked(head_parts[0], head_parts[1], head_parts[2], segment_row), per_head)
    attended = low_back(low(attended))
    attended = attended.transpose(1, 0, 2).reshape(ROW_LEN, D)
    branch = low_back(jnp.dot(attended, w_out, precision=HIGHEST) + out_bias)
    residual = tokens_row + branch
    normed_two = low(layer_norm(residual, ln2_gain, ln2_bias))
    pre_act = low_back(jnp.dot(normed_two, w_up, precision=HIGHEST) + up_bias)
    activated = low(jax.nn.gelu(pre_act, approximate=False))
    return residual + low_back(jnp.dot(activated, w_down, precision=HIGHEST) + down_bias)

def reference(tokens, segments, ln1_gain, ln1_bias, w_qkv, q_bias, v_bias, w_out, out_bias, ln2_gain, ln2_bias, w_up, up_bias, w_down, down_bias, cotangent):
    weights_in = tuple((weight.astype(jnp.float32) for weight in (ln1_gain, ln1_bias, w_qkv, q_bias, v_bias, w_out, out_bias, ln2_gain, ln2_bias, w_up, up_bias, w_down, down_bias)))

    def row_step(grad_sums, row_args):
        tokens_row, segment_row, cot_row = row_args

        def closed(tokens_now, *params):
            return row_forward(tokens_now, segment_row, *params)
        output_row, pullback = jax.vjp(closed, tokens_row.astype(jnp.float32), *weights_in)
        row_grads = pullback(cot_row.astype(jnp.float32))
        grad_sums = tuple((left_part + right_part for left_part, right_part in zip(grad_sums, row_grads[1:])))
        return (grad_sums, (output_row.astype(jnp.bfloat16), row_grads[0].astype(jnp.bfloat16)))
    zero_grads = tuple((jnp.zeros(weight.shape, jnp.float32) for weight in weights_in))
    grad_sums, (outputs, token_grads) = lax.scan(row_step, zero_grads, (tokens, segments, cotangent))
    factor = 1.0 / math.sqrt(ROWS * ROW_LEN)
    scaled = [entry * factor for entry in grad_sums]
    return (outputs, token_grads, scaled[0], scaled[1], scaled[2], scaled[3], scaled[4], scaled[5], scaled[6], scaled[7], scaled[8], scaled[9], scaled[10], scaled[11], scaled[12])
```

```python
import math
from functools import partial

import jax
import jax.numpy as jnp
from jax import lax
from jax.experimental import pallas as pl
from jax.experimental.pallas import tpu as pltpu
from jax.sharding import PartitionSpec as P

HEADS = 20
SEG_MOST = 1024
NORM_EPS = 1e-05
F32 = jnp.float32
BF16 = jnp.bfloat16
LOG2E = 1.4426950408889634
LN2 = 0.6931471805599453
FAR = -1e30
LANES = 128
TILE = 128
GROUP = 3
FEATURE = 96
VMEM_LIMIT = 60 * 1024 * 1024


def bits_of(size):
    return size.bit_length() - 1


def swap(value, axis, mask):
    size = lax.axis_size(axis)
    return lax.ppermute(value, axis, [(i, i ^ mask) for i in range(size)])


def gather_all(block):
    rows, seq = lax.axis_size("rows"), lax.axis_size("seq")
    stages = [("seq", b) for b in reversed(range(bits_of(seq)))]
    stages += [("rows", b) for b in reversed(range(bits_of(rows)))]
    place = 0
    for weight, (axis, bit) in enumerate(stages):
        place = place + (((lax.axis_index(axis) >> bit) & 1) << weight)
    total = rows * seq
    held = jnp.zeros((total,) + block.shape, block.dtype)
    held = lax.dynamic_update_index_in_dim(held, block, place, 0)
    for weight, (axis, bit) in enumerate(stages):
        width = 1 << weight
        mine = (place >> weight) << weight
        other = mine ^ width
        got = swap(lax.dynamic_slice_in_dim(held, mine, width, 0), axis, 1 << bit)
        held = lax.dynamic_update_slice_in_dim(held, got, other, 0)
    count = len(stages)
    held = held.reshape((2,) * count + block.shape)
    dims = []
    for axis, size in (("rows", rows), ("seq", seq)):
        for b in reversed(range(bits_of(size))):
            dims.append(count - 1 - stages.index((axis, b)))
    dims += list(range(count, count + block.ndim))
    return held.transpose(dims).reshape((rows, seq) + block.shape)


def scatter_sum(parts):
    rows, seq = lax.axis_size("rows"), lax.axis_size("seq")
    rb, sb = bits_of(rows), bits_of(seq)
    tail = parts.shape[2:]
    parts = parts.reshape((2,) * (rb + sb) + tail)
    dims = list(reversed(range(rb))) + [rb + d for d in reversed(range(sb))]
    dims += list(range(rb + sb, rb + sb + len(tail)))
    parts = parts.transpose(dims)
    for axis, count in (("rows", rb), ("seq", sb)):
        for b in range(count):
            bit = (lax.axis_index(axis) >> b) & 1
            keep = lax.dynamic_index_in_dim(parts, bit, 0, keepdims=False)
            send = lax.dynamic_index_in_dim(parts, 1 - bit, 0, keepdims=False)
            got = swap(send, axis, 1 << b)
            parts = (keep.astype(F32) + got.astype(F32)).astype(BF16)
    return parts


def sum_all(value):
    for axis in ("rows", "seq"):
        for b in range(bits_of(lax.axis_size(axis))):
            value = value + swap(value, axis, 1 << b)
    return value


def pad_heads(value, axis, heads):
    groups = -(-heads // GROUP)
    shape = value.shape
    width = shape[axis] // heads
    value = value.reshape(shape[:axis] + (heads, width) + shape[axis + 1 :])
    pads = [(0, 0)] * value.ndim
    pads[axis] = (0, groups * GROUP - heads)
    value = jnp.pad(value, pads)
    value = value.reshape(shape[:axis] + (groups, GROUP * width) + shape[axis + 1 :])
    pads = [(0, 0)] * value.ndim
    pads[axis + 1] = (0, LANES - GROUP * width)
    value = jnp.pad(value, pads)
    return value.reshape(shape[:axis] + (groups * LANES,) + shape[axis + 1 :])


def drop_pad(value, axis, heads, width):
    groups = -(-heads // GROUP)
    shape = value.shape
    value = value.reshape(shape[:axis] + (groups, LANES) + shape[axis + 1 :])
    value = lax.slice_in_dim(value, 0, GROUP * width, axis=axis + 1)
    value = value.reshape(shape[:axis] + (groups * GROUP * width,) + shape[axis + 1 :])
    return lax.slice_in_dim(value, 0, heads * width, axis=axis)


def dot(a, b):
    return jnp.dot(a, b, preferred_element_type=F32)


def dot_nt(a, b):
    return lax.dot_general(a, b, (((1,), (1,)), ((), ())), preferred_element_type=F32)


def dot_tn(a, b):
    return lax.dot_general(a, b, (((0,), (0,)), ((), ())), preferred_element_type=F32)


def qkv_kernel(
    where_ref, tok_ref, segc_ref, segr_ref, gain_ref, bias_ref, wrow_ref, brow_ref, wcol_ref,
    bcol_ref, krow_ref, vrow_ref, qrow_ref, kt_ref, vt_ref, qt_ref, *, scale,
):
    wide = krow_ref.shape[-1]
    width = kt_ref.shape[-2]
    x = tok_ref[0, 0].astype(F32)
    centre = jnp.mean(x, axis=-1, keepdims=True)
    x = x - centre
    inverse = lax.rsqrt(jnp.mean(x * x, axis=-1, keepdims=True) + NORM_EPS)
    normed = (x * inverse * gain_ref[...] + bias_ref[...]).astype(BF16)
    span = normed.shape[0]
    lane = lax.broadcasted_iota(jnp.int32, (span, wide), 1) % LANES
    kfeat = jnp.where(lane - FEATURE == segc_ref[0], 1.0, 0.0)
    rows = dot(normed, wrow_ref[...]) + brow_ref[...]
    qrow_ref[0] = (rows[:, :wide] * scale).astype(BF16)
    krow_ref[0] = (rows[:, wide : 2 * wide] + kfeat).astype(BF16)
    vrow_ref[0] = rows[:, 2 * wide :].astype(BF16)
    cols = dot_nt(wcol_ref[...], normed) + bcol_ref[...]
    row = lax.broadcasted_iota(jnp.int32, (wide, span), 0) % LANES - FEATURE
    qfeat = jnp.where((row >= 0) & (row != segr_ref[0]), FAR, 0.0)
    qt_ref[0] = (cols[:wide] * scale + qfeat).astype(BF16)
    kt_ref[0] = cols[wide : wide + width].astype(BF16)
    vt_ref[0] = cols[wide + width :].astype(BF16)


def head_rows(h):
    row = lax.broadcasted_iota(jnp.int32, (LANES, TILE), 0)
    return (row // 32 == h % GROUP) | (row >= FEATURE)


def head_lanes(h):
    lane = lax.broadcasted_iota(jnp.int32, (TILE, LANES), 1)
    return (lane // 32 == h % GROUP) | (lane >= FEATURE)


def lanes_of(h):
    return slice((h // GROUP) * LANES, (h // GROUP + 1) * LANES)


def attend_kernel(
    first_ref, last_ref, krow_ref, vt_ref, qt_ref, out_ref, lse_ref, qpad, top, total, acc, *, heads
):
    row_at = pl.program_id(0)
    tiles = out_ref.shape[-1] // TILE

    @pl.loop(0, tiles)
    def _(t):
        here = pl.ds(pl.multiple_of(t * TILE, TILE), TILE)
        for h in range(heads):
            block = qt_ref[0, lanes_of(h), here]
            qpad[h] = jnp.where(head_rows(h), block, jnp.zeros_like(block))
        top[...] = jnp.full_like(top, 2.0 * FAR)
        total[...] = jnp.zeros_like(total)
        acc[...] = jnp.zeros_like(acc)

        @pl.loop(first_ref[row_at, t], last_ref[row_at, t] + 1)
        def _(u):
            there = pl.ds(pl.multiple_of(u * TILE, TILE), TILE)
            for h in range(heads):
                mine = slice(h * 32, h * 32 + 32)
                scores = dot(krow_ref[0, there, lanes_of(h)], qpad[h])
                old = top[h : h + 1]
                new = jnp.maximum(old, jnp.max(scores, axis=0, keepdims=True))
                fade = jnp.exp2(old - new)
                probs = jnp.exp2(scores - new)
                top[h : h + 1] = new
                total[h : h + 1] = total[h : h + 1] * fade + jnp.sum(probs, axis=0, keepdims=True)
                acc[mine] = acc[mine] * fade + dot(vt_ref[0, mine, there], probs.astype(BF16))

        for h in range(heads):
            mine = slice(h * 32, h * 32 + 32)
            out_ref[0, mine, here] = (acc[mine] / total[h : h + 1]).astype(BF16)
        lse_ref[0, :, here] = top[...] + jnp.log2(jnp.maximum(total[...], 1e-37))


def back_kernel(
    first_ref, last_ref, krow_ref, vrow_ref, qrow_ref, kt_ref, qt_ref, grow_ref, gt_ref, lse_ref,
    delta_ref, dqt_ref, dkrow_ref, dvrow_ref, qpad, gpad, qlanes, glanes, klanes, vlanes, dk_acc,
    dv_acc, dq_acc, dk_far, dv_far, *, heads, start,
):
    row_at = pl.program_id(0)
    tiles = dqt_ref.shape[-1] // TILE
    groups = dk_acc.shape[-1] // LANES
    scale = 1.0 / math.sqrt(32.0)
    dk_acc[...] = jnp.zeros_like(dk_acc)
    dv_acc[...] = jnp.zeros_like(dv_acc)
    qlanes[...] = jnp.zeros_like(qlanes)
    glanes[...] = jnp.zeros_like(glanes)

    @pl.loop(0, tiles)
    def _(t):
        own = pl.ds(pl.multiple_of(t * TILE, TILE), TILE)
        here = pl.ds(pl.multiple_of((start + t) * TILE, TILE), TILE)
        first, last = first_ref[row_at, t], last_ref[row_at, t]
        for h in range(heads):
            spot = slice((h % GROUP) * TILE, (h % GROUP + 1) * TILE)
            keep = head_rows(h)
            block = qt_ref[0, lanes_of(h), here]
            qpad[h] = jnp.where(keep, block, jnp.zeros_like(block))
            block = gt_ref[0, lanes_of(h), here]
            gpad[h] = jnp.where(keep, block, jnp.zeros_like(block))
            keep = head_lanes(h)
            block = qrow_ref[0, here, lanes_of(h)]
            qlanes[h // GROUP, spot] = jnp.where(keep, block, jnp.zeros_like(block))
            block = grow_ref[0, here, lanes_of(h)]
            glanes[h // GROUP, spot] = jnp.where(keep, block, jnp.zeros_like(block))
        dq_acc[...] = jnp.zeros_like(dq_acc)

        def pair(there, h):
            scores = dot(krow_ref[0, there, lanes_of(h)], qpad[h])
            probs = jnp.exp2(scores - lse_ref[0, h : h + 1, here])
            slope = dot(vrow_ref[0, there, lanes_of(h)], gpad[h])
            ds = (probs * (slope - delta_ref[0, h : h + 1, here])).astype(BF16)
            mine = slice(h * 32, h * 32 + 32)
            dq_acc[mine] += dot(kt_ref[0, mine, there], ds)
            return probs.astype(BF16), ds

        @pl.loop(jnp.maximum(first, start), jnp.minimum(last, start + tiles - 1) + 1)
        def _(u):
            there = pl.ds(pl.multiple_of(u * TILE, TILE), TILE)
            local = pl.ds(pl.multiple_of((u - start) * TILE, TILE), TILE)
            for g in range(groups):
                members = [h for h in range(heads) if h // GROUP == g]
                both = [pair(there, h) for h in members]
                depth = len(members) * TILE
                lanes = slice(g * LANES, (g + 1) * LANES)
                dv_acc[local, lanes] += dot(
                    jnp.concatenate([b[0] for b in both], axis=1), glanes[g, :depth]
                )
                dk_acc[local, lanes] += dot(
                    jnp.concatenate([b[1] for b in both], axis=1), qlanes[g, :depth]
                )

        @pl.when((first < start) | (last >= start + tiles))
        def _():
            for h in range(heads):
                keep = head_lanes(h)
                block = krow_ref[0, here, lanes_of(h)]
                klanes[h] = jnp.where(keep, block, jnp.zeros_like(block))
                block = vrow_ref[0, here, lanes_of(h)]
                vlanes[h] = jnp.where(keep, block, jnp.zeros_like(block))
            dk_far[...] = jnp.zeros_like(dk_far)
            dv_far[...] = jnp.zeros_like(dv_far)

            def far(u):
                there = pl.ds(pl.multiple_of(u * TILE, TILE), TILE)
                for h in range(heads):
                    pair(there, h)
                    scores = dot(klanes[h], qt_ref[0, lanes_of(h), there])
                    probs = jnp.exp2(scores - lse_ref[0, h : h + 1, there])
                    slope = dot(vlanes[h], gt_ref[0, lanes_of(h), there])
                    ds = (probs * (slope - delta_ref[0, h : h + 1, there])).astype(BF16)
                    dv_far[h] += dot(probs.astype(BF16), grow_ref[0, there, lanes_of(h)])
                    dk_far[h] += dot(ds, qrow_ref[0, there, lanes_of(h)])

            pl.loop(first, jnp.minimum(start, last + 1))(far)
            pl.loop(jnp.maximum(start + tiles, first), last + 1)(far)
            for h in range(heads):
                keep = head_lanes(h)
                dv_acc[own, lanes_of(h)] += jnp.where(keep, dv_far[h], 0.0)
                dk_acc[own, lanes_of(h)] += jnp.where(keep, dk_far[h], 0.0)

        dqt_ref[0, :, own] = (dq_acc[...] * scale).astype(BF16)

    dkrow_ref[0] = (dk_acc[...] * LN2).astype(BF16)
    dvrow_ref[0] = dv_acc[...].astype(BF16)


def feed_kernel(
    norm_ref, cot_ref, up_ref, down_ref, bias_ref, out_ref, back_ref, gup_ref, gdown_ref, gbias_ref,
    out_acc, back_acc, gup_acc, gdown_acc, gbias_acc, *, chunk,
):
    k, j = pl.program_id(0), pl.program_id(1)
    here = pl.ds(pl.multiple_of(j * chunk, chunk), chunk)
    norm, cot = norm_ref[0], cot_ref[0]
    up, down = up_ref[here, :], down_ref[here, :]
    pre = dot_nt(norm, up) + bias_ref[...]
    phi = 0.5 + 0.5 * lax.erf(pre * (1.0 / math.sqrt(2.0)))
    dens = jnp.exp(-0.5 * pre * pre) * (1.0 / math.sqrt(2.0 * math.pi))
    act = (pre * phi).astype(BF16)
    slope = dot_nt(cot, down) * (phi + pre * dens)
    slope_low = slope.astype(BF16)

    @pl.when(j == 0)
    def _():
        out_acc[...] = dot(act, down)
        back_acc[...] = dot(slope_low, up)

    @pl.when(j > 0)
    def _():
        out_acc[...] += dot(act, down)
        back_acc[...] += dot(slope_low, up)

    bias_sum = jnp.sum(slope_low.astype(F32), axis=0, keepdims=True)
    gup, gdown = dot_tn(slope_low, norm), dot_tn(act, cot)

    @pl.when(k == 0)
    def _():
        gup_acc[here, :] = gup
        gdown_acc[here, :] = gdown
        gbias_acc[pl.ds(j, 1)] = bias_sum

    @pl.when(k > 0)
    def _():
        gup_acc[here, :] += gup
        gdown_acc[here, :] += gdown
        gbias_acc[pl.ds(j, 1)] += bias_sum

    @pl.when(j == pl.num_programs(1) - 1)
    def _():
        out_ref[0] = out_acc[...].astype(BF16)
        back_ref[0] = back_acc[...].astype(BF16)

    @pl.when(k == pl.num_programs(0) - 1)
    def _():
        gup_ref[...] = gup_acc[here, :].astype(BF16)
        gdown_ref[...] = gdown_acc[here, :].astype(BF16)
        gbias_ref[0] = gbias_acc[pl.ds(j, 1)]


def norm_stats(value):
    centre = jnp.mean(value, axis=-1, keepdims=True)
    centred = value - centre
    inverse = lax.rsqrt(jnp.mean(centred * centred, axis=-1, keepdims=True) + NORM_EPS)
    return centred * inverse, inverse


def norm_back(upstream, unit_rows, inverse, gain):
    scaled = upstream * gain
    centred_mean = jnp.mean(scaled, axis=-1, keepdims=True)
    along_unit = jnp.mean(scaled * unit_rows, axis=-1, keepdims=True)
    return inverse * (scaled - centred_mean - unit_rows * along_unit)


def on_device(
    tokens, segments, ln1_gain, ln1_bias, w_qkv, q_bias, v_bias, w_out, out_bias, ln2_gain,
    ln2_bias, w_up, up_bias, w_down, down_bias, cotangent,
):
    nrow, span, model = tokens.shape
    rows, seq = lax.axis_size("rows"), lax.axis_size("seq")
    count = nrow * span
    width = model // HEADS
    ri, si = lax.axis_index("rows"), lax.axis_index("seq")
    grad_scale = 1.0 / math.sqrt(rows * nrow * seq * span)
    params = partial(pltpu.CompilerParams, vmem_limit_bytes=VMEM_LIMIT)

    team = max(g for g in (1, 2, 4) if HEADS % g == 0 and seq % g == 0 and g * span <= SEG_MOST)
    chunks, chunk = seq // team, team * span
    halo = -(-(SEG_MOST - 1) // chunk)
    blocks = (2 * halo + 1) * team
    window = blocks * span
    heads = HEADS // team
    here = heads * width
    groups = -(-heads // GROUP)
    wide = groups * LANES
    member = si % team

    def fetch(value_for, dc, k):
        perm = []
        for c in range(chunks):
            for m in range(team):
                if 0 <= c + dc < chunks:
                    perm.append(((c + dc) * team + (m + k) % team, c * team + m))
        value = value_for((member - k) % team)
        if dc == 0 and k == 0:
            return value
        return lax.ppermute(value, "seq", perm)

    def fetch_window(value_for):
        got = [fetch(value_for, dc, k) for dc in range(-halo, halo + 1) for k in range(team)]
        return jnp.stack(got)

    def in_order(rotated, axis):
        if team == 1:
            return rotated[0]
        twice = jnp.concatenate(list(rotated) * 2, axis=axis)
        size = rotated[0].shape[axis]
        return lax.dynamic_slice_in_dim(twice, ((team - member) % team) * size, team * size, axis)

    qkv_full = gather_all(w_qkv).transpose(0, 2, 1, 3).reshape(model, 3 * model)
    tok_rot = fetch_window(lambda m: tokens)
    seg_rot = fetch_window(lambda m: segments + 1)
    order = jnp.arange(blocks, dtype=jnp.int32)
    source = (order // team) * team + (order % team - member) % team
    segs = seg_rot[source].transpose(1, 0, 2).reshape(nrow, window)

    out_full = lax.all_gather(w_out, ("rows", "seq"), axis=0, tiled=False)
    out_full = out_full.reshape(rows, seq, model // rows, model // seq)
    out_full = out_full.transpose(0, 2, 1, 3).reshape(model, model)

    ff = up_bias.shape[0]
    hid = ff // rows
    part = ff // (rows * seq)
    both = jnp.stack([w_up.T, w_down])
    both = both.reshape(2, rows, part, model // rows)
    slices = [
        (ri ^ k, swap(lax.dynamic_index_in_dim(both, ri ^ k, 1, keepdims=False), "rows", k) if k else
         lax.dynamic_index_in_dim(both, ri, 1, keepdims=False))
        for k in range(rows)
    ]
    mine = jnp.zeros((rows, 2, part, model // rows), BF16)
    for at, piece in slices:
        mine = lax.dynamic_update_index_in_dim(mine, piece, at, 0)
    mine = mine.transpose(1, 2, 0, 3).reshape(2, part, model)
    feed_w = lax.all_gather(mine, "seq", axis=1, tiled=False).reshape(2, hid, model)
    my_up_bias = lax.dynamic_index_in_dim(
        up_bias.astype(F32).reshape(seq, rows, part), ri, 1, keepdims=False
    ).reshape(1, hid)

    cot_low = cotangent.reshape(count, model)
    cot_all = jnp.stack([swap(cot_low, "rows", k) if k else cot_low for k in range(rows)])

    gain_one, gain_two = ln1_gain.astype(F32)[None], ln2_gain.astype(F32)[None]
    shift_one, shift_two = ln1_bias.astype(F32)[None], ln2_bias.astype(F32)[None]
    my_w = lax.dynamic_index_in_dim(
        qkv_full.reshape(model, 3, team, here), member, 2, keepdims=False
    )
    qb = lax.dynamic_index_in_dim(q_bias.astype(F32).reshape(team, here), member, 0, keepdims=False)
    vb = lax.dynamic_index_in_dim(v_bias.astype(F32).reshape(team, here), member, 0, keepdims=False)
    pad_w = [pad_heads(my_w[:, i], 1, heads) for i in range(3)]
    pad_qb, pad_vb = pad_heads(qb, 0, heads), pad_heads(vb, 0, heads)
    w_row = jnp.concatenate(pad_w, axis=1)
    b_row = jnp.concatenate([pad_qb, jnp.zeros_like(pad_qb), pad_vb])[None]
    w_col = jnp.concatenate([pad_w[0], my_w[:, 1], my_w[:, 2]], axis=1).T
    b_col = jnp.concatenate([pad_qb, jnp.zeros_like(qb), vb])[:, None]

    whole = lambda *shape: pl.BlockSpec(shape, lambda *_: (0,) * len(shape))
    row_spec = pl.BlockSpec((1, span, wide), lambda r, b, s: (r, b, 0))
    col_spec = lambda size: pl.BlockSpec((1, size, span), lambda r, b, s: (r, 0, b))
    row_shape = jax.ShapeDtypeStruct((nrow, window, wide), BF16)
    col_shape = lambda size: jax.ShapeDtypeStruct((nrow, size, window), BF16)
    krow, vrow, qrow, kt, vt, qt = pl.pallas_call(
        partial(qkv_kernel, scale=LOG2E / math.sqrt(width)),
        grid_spec=pltpu.PrefetchScalarGridSpec(
            num_scalar_prefetch=1,
            grid=(nrow, blocks),
            in_specs=[
                pl.BlockSpec((1, 1, span, model), lambda r, b, s: (s[b], r, 0, 0)),
                pl.BlockSpec((1, span, 1), lambda r, b, s: (r, b, 0)),
                pl.BlockSpec((1, 1, span), lambda r, b, s: (r, 0, b)),
                whole(1, model), whole(1, model), whole(model, 3 * wide), whole(1, 3 * wide),
                whole(wide + 2 * here, model), whole(wide + 2 * here, 1),
            ],
            out_specs=[row_spec] * 3 + [col_spec(here), col_spec(here), col_spec(wide)],
        ),
        out_shape=[row_shape] * 3 + [col_shape(here), col_shape(here), col_shape(wide)],
        compiler_params=params(),
        name="qkv",
    )(source, tok_rot, segs[:, :, None], segs[:, None, :], gain_one, shift_one, w_row, b_row, w_col, b_col)

    tiles, start = chunk // TILE, halo * chunk // TILE
    own_segs = lax.slice_in_dim(segs, halo * chunk, (halo + 1) * chunk, axis=1)
    own_segs = own_segs.reshape(nrow, tiles, TILE)
    at = jnp.arange(window, dtype=jnp.int32)
    first = jnp.min(
        jnp.where(segs[:, None, :] == own_segs[:, :, :1], at, window), axis=-1
    ) // TILE
    last = jnp.max(jnp.where(segs[:, None, :] == own_segs[:, :, -1:], at, 0), axis=-1) // TILE

    once = pl.Buffered(1)
    per_row = lambda *shape: pl.BlockSpec(
        (1,) + shape, lambda r, *_: (r,) + (0,) * len(shape), pipeline_mode=once
    )
    stat = -(-heads // 8) * 8
    attended_t, lse = pl.pallas_call(
        partial(attend_kernel, heads=heads),
        grid_spec=pltpu.PrefetchScalarGridSpec(
            num_scalar_prefetch=2,
            grid=(nrow,),
            in_specs=[
                per_row(window, wide), per_row(here, window),
                pl.BlockSpec((1, wide, chunk), lambda r, *_: (r, 0, halo), pipeline_mode=once),
            ],
            out_specs=[per_row(here, chunk), per_row(stat, chunk)],
            scratch_shapes=[
                pltpu.VMEM((heads, LANES, TILE), BF16), pltpu.VMEM((stat, TILE), F32),
                pltpu.VMEM((stat, TILE), F32), pltpu.VMEM((here, TILE), F32),
            ],
        ),
        out_shape=[
            jax.ShapeDtypeStruct((nrow, here, chunk), BF16),
            jax.ShapeDtypeStruct((nrow, stat, chunk), F32),
        ],
        compiler_params=params(),
        name="attend",
    )(first, last, krow, vt, qt)

    by_member = attended_t.reshape(nrow, here, team, span)
    joined = in_order(
        [
            fetch(lambda m: lax.dynamic_index_in_dim(by_member, m, 2, keepdims=False), 0, k)
            for k in range(team)
        ],
        1,
    )
    attended = joined.transpose(0, 2, 1).reshape(count, model)
    lse_parts = []
    for dc in range(-halo, halo + 1):
        if dc == 0:
            lse_parts.append(lse)
        else:
            perm = [
                ((c + dc) * team + m, c * team + m)
                for c in range(chunks) for m in range(team) if 0 <= c + dc < chunks
            ]
            lse_parts.append(lax.ppermute(lse, "seq", perm))
    lse_window = jnp.concatenate(lse_parts, axis=2)

    flat_tokens = tokens.reshape(count, model).astype(F32)
    residual = flat_tokens + dot(attended, out_full) + out_bias.astype(F32)
    unit_two, inverse_two = norm_stats(residual)
    normed_two = (unit_two * gain_two + shift_two).astype(BF16)

    norm_all = jnp.stack([swap(normed_two, "rows", k) if k else normed_two for k in range(rows)])
    step = 256 if hid % 256 == 0 else LANES
    tok_spec = pl.BlockSpec((1, count, model), lambda k, j: (k, 0, 0))
    grad_spec = pl.BlockSpec((step, model), lambda k, j: (jnp.where(k == rows - 1, j, 0), 0))
    out_parts, back_parts, grad_up, grad_down, grad_up_bias = pl.pallas_call(
        partial(feed_kernel, chunk=step),
        grid=(rows, hid // step),
        in_specs=[
            tok_spec, tok_spec,
            whole(hid, model), whole(hid, model),
            pl.BlockSpec((1, step), lambda k, j: (0, j)),
        ],
        out_specs=[
            tok_spec, tok_spec, grad_spec, grad_spec,
            pl.BlockSpec((1, 1, step), lambda k, j: (jnp.where(k == rows - 1, j, 0), 0, 0)),
        ],
        out_shape=[
            jax.ShapeDtypeStruct((rows, count, model), BF16),
            jax.ShapeDtypeStruct((rows, count, model), BF16),
            jax.ShapeDtypeStruct((hid, model), BF16),
            jax.ShapeDtypeStruct((hid, model), BF16),
            jax.ShapeDtypeStruct((hid // step, 1, step), F32),
        ],
        scratch_shapes=[
            pltpu.VMEM((count, model), F32), pltpu.VMEM((count, model), F32),
            pltpu.VMEM((hid, model), F32), pltpu.VMEM((hid, model), F32),
            pltpu.VMEM((hid // step, step), F32),
        ],
        compiler_params=params(),
        name="feed",
    )(norm_all, cot_all, feed_w[0], feed_w[1], my_up_bias)

    normed_two_grad = back_parts[0].astype(F32)
    for k in range(1, rows):
        normed_two_grad = normed_two_grad + swap(back_parts[k], "rows", k).astype(F32)
    result = residual + down_bias.astype(F32) + out_parts[0].astype(F32)
    for k in range(1, rows):
        result = result + swap(out_parts[k], "rows", k).astype(F32)
    output = result.astype(BF16).reshape(tokens.shape)

    feed_grad = jnp.stack(
        [grad_up.reshape(seq, part, model), grad_down.reshape(seq, part, model)], axis=1
    )
    feed_sum = lax.psum_scatter(feed_grad, "seq", scatter_dimension=0, tiled=False)
    feed_sum = feed_sum.reshape(2, part, rows, model // rows)
    back = jnp.zeros((rows, 2, part, model // rows), BF16)
    for k in range(rows):
        piece = lax.dynamic_index_in_dim(feed_sum, ri ^ k, 2, keepdims=False)
        piece = swap(piece, "rows", k) if k else piece
        back = lax.dynamic_update_index_in_dim(back, piece, ri ^ k, 0)
    back = back.transpose(1, 0, 2, 3).reshape(2, ff // seq, model // rows).astype(F32) * grad_scale
    sum_up, sum_down = back[0].T, back[1]

    cot_wide = cot_low.astype(F32)
    grad_gain_two = jnp.sum(normed_two_grad * unit_two, axis=0)
    grad_shift_two = jnp.sum(normed_two_grad, axis=0)
    residual_grad = cot_wide + norm_back(normed_two_grad, unit_two, inverse_two, gain_two)
    branch_grad = residual_grad.astype(BF16)
    grad_out = dot_tn(attended, branch_grad)
    grad_out_bias = jnp.sum(branch_grad, axis=0, dtype=F32)
    attended_grad = dot_nt(branch_grad, out_full).astype(BF16)

    grad_out = grad_out.astype(BF16).reshape(rows, model // rows, seq, model // seq)
    grad_out = grad_out.transpose(0, 2, 1, 3).reshape(rows * seq, model // rows, model // seq)
    sum_out = lax.psum_scatter(grad_out, ("rows", "seq"), scatter_dimension=0, tiled=False)
    sum_out = sum_out.astype(F32) * grad_scale

    wide_bias = jnp.zeros((seq, rows, part), F32)
    wide_bias = lax.dynamic_update_index_in_dim(
        wide_bias, grad_up_bias.reshape(seq, part), ri, 1
    ).reshape(ff)
    early = lax.psum(
        jnp.concatenate([
            grad_out_bias, grad_gain_two, grad_shift_two,
            jnp.sum(cot_low, axis=0, dtype=F32), wide_bias,
        ]),
        ("rows", "seq"),
    ) * grad_scale
    sum_out_bias, sum_gain_two, sum_shift_two, sum_down_bias = (
        early[i * model : (i + 1) * model] for i in range(4)
    )
    sum_up_bias = early[4 * model :]

    delta = jnp.sum(
        (attended.astype(F32) * attended_grad.astype(F32)).reshape(nrow, span, HEADS, width), axis=-1
    ).transpose(0, 2, 1)
    delta = jnp.pad(delta.reshape(nrow, team, heads, span), ((0, 0), (0, 0), (0, stat - heads), (0, 0)))
    grad_members = attended_grad.reshape(nrow, span, team, here)
    grad_rot = fetch_window(lambda m: lax.dynamic_index_in_dim(grad_members, m, 2, keepdims=False))
    delta_rot = fetch_window(lambda m: lax.dynamic_index_in_dim(delta, m, 1, keepdims=False))
    grad_win = grad_rot[source].transpose(1, 0, 2, 3).reshape(nrow, window, here)
    delta_win = delta_rot[source].transpose(1, 2, 0, 3).reshape(nrow, stat, window)
    grow = pad_heads(grad_win, 2, heads)
    gt = grow.transpose(0, 2, 1)

    dqt, dkrow, dvrow = pl.pallas_call(
        partial(back_kernel, heads=heads, start=start),
        grid_spec=pltpu.PrefetchScalarGridSpec(
            num_scalar_prefetch=2,
            grid=(nrow,),
            in_specs=[
                per_row(window, wide), per_row(window, wide), per_row(window, wide),
                per_row(here, window), per_row(wide, window), per_row(window, wide),
                per_row(wide, window), per_row(stat, window), per_row(stat, window),
            ],
            out_specs=[per_row(here, chunk), per_row(chunk, wide), per_row(chunk, wide)],
            scratch_shapes=[
                pltpu.VMEM((heads, LANES, TILE), BF16), pltpu.VMEM((heads, LANES, TILE), BF16),
                pltpu.VMEM((groups, GROUP * TILE, LANES), BF16),
                pltpu.VMEM((groups, GROUP * TILE, LANES), BF16),
                pltpu.VMEM((heads, TILE, LANES), BF16), pltpu.VMEM((heads, TILE, LANES), BF16),
                pltpu.VMEM((chunk, wide), F32), pltpu.VMEM((chunk, wide), F32),
                pltpu.VMEM((here, TILE), F32),
                pltpu.VMEM((heads, TILE, LANES), F32), pltpu.VMEM((heads, TILE, LANES), F32),
            ],
        ),
        out_shape=[
            jax.ShapeDtypeStruct((nrow, here, chunk), BF16),
            jax.ShapeDtypeStruct((nrow, chunk, wide), BF16),
            jax.ShapeDtypeStruct((nrow, chunk, wide), BF16),
        ],
        compiler_params=params(),
        name="attend_back",
    )(first, last, krow, vrow, qrow, kt, qt, grow, gt, lse_window, delta_win)

    mixed = jnp.concatenate(
        [dqt.transpose(0, 2, 1), drop_pad(dkrow, 2, heads, width), drop_pad(dvrow, 2, heads, width)],
        axis=2,
    )
    mixed_flat = mixed.reshape(nrow * chunk, 3 * here)
    chunk_tokens = in_order([tok_rot[halo * team + k] for k in range(team)], 1)
    chunk_unit, _ = norm_stats(chunk_tokens.astype(F32).reshape(nrow * chunk, model))
    chunk_norm = (chunk_unit * gain_one + shift_one).astype(BF16)
    grad_qkv = dot_tn(chunk_norm, mixed_flat).astype(BF16)
    bias_sums = jnp.sum(mixed_flat, axis=0, dtype=F32).reshape(3, here)
    back_part = dot_nt(mixed_flat, my_w.reshape(model, 3 * here)).astype(BF16)
    back_members = back_part.reshape(nrow, team, span, model)
    normed_one_grad = 0.0
    for k in range(team):
        normed_one_grad = normed_one_grad + fetch(
            lambda m: lax.dynamic_index_in_dim(back_members, m, 1, keepdims=False), 0, k
        ).astype(F32)
    normed_one_grad = normed_one_grad.reshape(count, model)
    unit_one, inverse_one = norm_stats(flat_tokens)
    grad_gain_one = jnp.sum(normed_one_grad * unit_one, axis=0)
    grad_shift_one = jnp.sum(normed_one_grad, axis=0)
    tokens_grad = residual_grad + norm_back(normed_one_grad, unit_one, inverse_one, gain_one)
    tokens_grad = tokens_grad.astype(BF16).reshape(tokens.shape)

    spread = jnp.zeros((model, 3, team, here), BF16)
    spread = lax.dynamic_update_index_in_dim(spread, grad_qkv.reshape(model, 3, here), member, 2)
    spread = spread.reshape(rows, model // rows, seq, 3 * model // seq).transpose(0, 2, 1, 3)
    sum_qkv = scatter_sum(spread).astype(F32) * grad_scale

    bias_full = jnp.zeros((2, team, here), F32)
    bias_full = lax.dynamic_update_index_in_dim(bias_full, bias_sums[0::2], member, 1)
    late = sum_all(
        jnp.concatenate([grad_gain_one, grad_shift_one, bias_full.reshape(2 * model)])
    ) * grad_scale
    sum_gain_one, sum_shift_one, sum_q_bias, sum_v_bias = (
        late[i * model : (i + 1) * model] for i in range(4)
    )

    return (
        output, tokens_grad, sum_gain_one, sum_shift_one, sum_qkv, sum_q_bias, sum_v_bias, sum_out,
        sum_out_bias, sum_gain_two, sum_shift_two, sum_up, sum_up_bias, sum_down, sum_down_bias,
    )


def solution(mesh):
    tok, mat, rep = P("rows", "seq", None), P("rows", "seq"), P()
    in_specs = (
        tok, mat, rep, rep, mat, rep, rep, mat, rep, rep, rep, mat, rep, P("seq", "rows"), rep, tok,
    )
    out_specs = (
        tok, tok, rep, rep, mat, rep, rep, mat, rep, rep, rep, mat, rep, P("seq", "rows"), rep,
    )
    return jax.shard_map(
        on_device, mesh=mesh, in_specs=in_specs, out_specs=out_specs, check_vma=False
    )
```

```python
import math
from functools import partial

import jax
import jax.numpy as jnp
from jax import lax
from jax.experimental import pallas as pl
from jax.experimental.pallas import tpu as pltpu
from jax.sharding import PartitionSpec as P

HEADS = 20
SEG_MOST = 1024
NORM_EPS = 1e-05
F32 = jnp.float32
BF16 = jnp.bfloat16
LOG2E = 1.4426950408889634
LN2 = 0.6931471805599453
FAR = -1e30
LANES = 128
TILE = 128
GROUP = 3
FEATURE = 96
VMEM_LIMIT = 60 * 1024 * 1024


def bits_of(size):
    return size.bit_length() - 1


def swap(value, axis, mask):
    size = lax.axis_size(axis)
    return lax.ppermute(value, axis, [(i, i ^ mask) for i in range(size)])


def exchange(pieces, axis):
    size, me = lax.axis_size(axis), lax.axis_index(axis)
    out = pieces
    for k in range(1, size):
        got = swap(lax.dynamic_index_in_dim(pieces, me ^ k, 0, keepdims=False), axis, k)
        out = lax.dynamic_update_index_in_dim(out, got, me ^ k, 0)
    return out


def gather_all(block):
    rows, seq = lax.axis_size("rows"), lax.axis_size("seq")
    stages = [("seq", b) for b in reversed(range(bits_of(seq)))]
    stages += [("rows", b) for b in reversed(range(bits_of(rows)))]
    place = 0
    for weight, (axis, bit) in enumerate(stages):
        place = place + (((lax.axis_index(axis) >> bit) & 1) << weight)
    total = rows * seq
    held = jnp.zeros((total,) + block.shape, block.dtype)
    held = lax.dynamic_update_index_in_dim(held, block, place, 0)
    for weight, (axis, bit) in enumerate(stages):
        width = 1 << weight
        mine = (place >> weight) << weight
        other = mine ^ width
        got = swap(lax.dynamic_slice_in_dim(held, mine, width, 0), axis, 1 << bit)
        held = lax.dynamic_update_slice_in_dim(held, got, other, 0)
    count = len(stages)
    held = held.reshape((2,) * count + block.shape)
    dims = []
    for axis, size in (("rows", rows), ("seq", seq)):
        for b in reversed(range(bits_of(size))):
            dims.append(count - 1 - stages.index((axis, b)))
    dims += list(range(count, count + block.ndim))
    return held.transpose(dims).reshape((rows, seq) + block.shape)


def scatter_sum(parts):
    rows, seq = lax.axis_size("rows"), lax.axis_size("seq")
    rb, sb = bits_of(rows), bits_of(seq)
    tail = parts.shape[2:]
    parts = parts.reshape((2,) * (rb + sb) + tail)
    dims = list(reversed(range(rb))) + [rb + d for d in reversed(range(sb))]
    dims += list(range(rb + sb, rb + sb + len(tail)))
    parts = parts.transpose(dims)
    for axis, count in (("rows", rb), ("seq", sb)):
        for b in range(count):
            bit = (lax.axis_index(axis) >> b) & 1
            keep = lax.dynamic_index_in_dim(parts, bit, 0, keepdims=False)
            send = lax.dynamic_index_in_dim(parts, 1 - bit, 0, keepdims=False)
            got = swap(send, axis, 1 << b)
            parts = (keep.astype(F32) + got.astype(F32)).astype(BF16)
    return parts


def sum_all(value):
    for axis in ("rows", "seq"):
        for b in range(bits_of(lax.axis_size(axis))):
            value = value + swap(value, axis, 1 << b)
    return value


def gather_orders(rows, seq):
    seq_bits = [("seq", b) for b in reversed(range(bits_of(seq)))]
    row_bits = [("rows", b) for b in reversed(range(bits_of(rows)))]
    return seq_bits + row_bits, row_bits[:-1] + seq_bits + row_bits[-1:]


def bit_at(value, bit):
    return value // (1 << bit) % 2


def flipped(value, bit):
    return value + (1 - 2 * bit_at(value, bit)) * (1 << bit)


def window_kernel(*refs, pays, units, team, chunks, halo, orders):
    total = pays + units
    ins, outs = refs[:total], refs[total : 2 * total]
    keep_sem, mate_send, mate_recv, far_send, far_recv = refs[2 * total : 2 * total + 5]
    rows, seq = lax.axis_size("rows"), lax.axis_size("seq")
    r, s = lax.axis_index("rows"), lax.axis_index("seq")
    c, m = s // team, s % team

    barrier = pltpu.get_barrier_semaphore()
    for j in range(1, seq):
        pl.semaphore_signal(barrier, inc=1, device_id={"seq": (s + j) % seq})
    if units:
        for j in range(1, rows):
            pl.semaphore_signal(barrier, inc=1, device_id={"rows": (r + j) % rows})
    pl.semaphore_wait(barrier, seq - 1 + (rows - 1) * units)

    def piece(p, member):
        return ins[p].at[member] if ins[p].shape[0] > 1 else ins[p].at[0]

    def mate(p, k):
        to = (m + k) % team
        return pltpu.make_async_remote_copy(
            src_ref=piece(p, to), dst_ref=outs[p].at[halo * team + m],
            send_sem=mate_send.at[p, k], recv_sem=mate_recv.at[p, k], device_id={"seq": c * team + to},
        )

    def mate_got(p, k):
        slot = outs[p].at[halo * team + (m + team - k) % team]
        return pltpu.make_async_remote_copy(
            src_ref=slot, dst_ref=slot, send_sem=mate_send.at[p, k], recv_sem=mate_recv.at[p, k],
            device_id={"seq": c * team + (m + k) % team},
        )

    steps = [d for n in range(1, halo + 1) for d in (-n, n)]

    def far(p, i, k):
        d, mm = steps[i], (m + team - k) % team
        src = piece(p, m) if k == 0 else outs[p].at[halo * team + mm]
        return pltpu.make_async_remote_copy(
            src_ref=src, dst_ref=outs[p].at[(halo - d) * team + mm],
            send_sem=far_send.at[p, i, k], recv_sem=far_recv.at[p, i, k],
            device_id={"seq": (c + d) * team + m},
        )

    def far_got(p, i, k):
        slot = outs[p].at[(halo - steps[i]) * team + (m + team - k) % team]
        return pltpu.make_async_remote_copy(
            src_ref=slot, dst_ref=slot, send_sem=far_send.at[p, i, k], recv_sem=far_recv.at[p, i, k],
            device_id={"seq": (c + steps[i]) * team + m},
        )

    def sends(i):
        return (c + steps[i] >= 0) & (c + steps[i] < chunks)

    def gets(i):
        return (c - steps[i] >= 0) & (c - steps[i] < chunks)

    def start_far(k):
        for i in range(len(steps)):
            @pl.when(sends(i))
            def _():
                for p in range(pays):
                    far(p, i, k).start()

    keeps = [
        pltpu.make_async_copy(piece(p, m), outs[p].at[halo * team + m], keep_sem.at[p])
        for p in range(pays)
    ]
    if units:
        unit_send, unit_recv = refs[2 * total + 5 :]
        unit_ref, unit_out = ins[-1], outs[-1]
        places = []
        for order in orders:
            place = 0
            for n, (axis, bit) in enumerate(order):
                place = place + bit_at(r if axis == "rows" else s, bit) * (1 << n)
            places.append(place)
            keeps.append(
                pltpu.make_async_copy(
                    unit_ref.at[len(places) - 1], unit_out.at[len(places) - 1, place],
                    keep_sem.at[pays + len(places) - 1],
                )
            )

        def stage(color, n):
            axis, bit = orders[color][n]
            width = 1 << n
            mine = places[color] // width * width
            group = unit_out.at[color, pl.ds(mine, width)]
            return pltpu.make_async_remote_copy(
                src_ref=group, dst_ref=group, send_sem=unit_send.at[color, n],
                recv_sem=unit_recv.at[color, n], device_id={axis: flipped(r if axis == "rows" else s, bit)},
            )

        def stage_got(color, n):
            axis, bit = orders[color][n]
            width = 1 << n
            group = unit_out.at[color, pl.ds(flipped(places[color] // width, 0) * width, width)]
            return pltpu.make_async_remote_copy(
                src_ref=group, dst_ref=group, send_sem=unit_send.at[color, n],
                recv_sem=unit_recv.at[color, n], device_id={axis: flipped(r if axis == "rows" else s, bit)},
            )

    for copy in keeps:
        copy.start()
    for k in range(1, team):
        for p in range(pays):
            mate(p, k).start()
    start_far(0)
    forwards = list(range(1, team))

    def forward():
        k = forwards.pop(0)
        for p in range(pays):
            mate_got(p, k).wait_recv()
        start_far(k)

    if units:
        for color in range(2):
            keeps[pays + color].wait()
            stage(color, 0).start()
        for n in range(1, len(orders[0])):
            for color in range(2):
                stage_got(color, n - 1).wait_recv()
                stage(color, n).start()
            if n >= 2 and forwards:
                forward()
    while forwards:
        forward()
    for p in range(pays):
        keeps[p].wait()
    for k in range(1, team):
        for p in range(pays):
            mate(p, k).wait_send()
    for i in range(len(steps)):
        for k in range(team):
            @pl.when(gets(i))
            def _():
                for p in range(pays):
                    far_got(p, i, k).wait_recv()

            @pl.when(sends(i))
            def _():
                for p in range(pays):
                    far(p, i, k).wait_send()
    if units:
        final = len(orders[0]) - 1
        for color in range(2):
            stage_got(color, final).wait_recv()
            for n in range(final + 1):
                stage(color, n).wait_send()


def window_of(payloads, unit, collective_id, *, team, chunks, halo, name):
    rows, seq = lax.axis_size("rows"), lax.axis_size("seq")
    orders = gather_orders(rows, seq)
    units = unit is not None
    blocks = (2 * halo + 1) * team
    shapes = [jax.ShapeDtypeStruct((blocks,) + p.shape[1:], p.dtype) for p in payloads]
    pays, steps, stages = len(payloads), 2 * halo, len(orders[0])
    sems = pltpu.SemaphoreType.DMA
    scratch = [
        sems((pays + 2,)), sems((pays, team)), sems((pays, team)), sems((pays, steps, team)),
        sems((pays, steps, team)),
    ]
    operands = list(payloads)
    if units:
        shapes.append(jax.ShapeDtypeStruct((2, rows * seq) + unit.shape[1:], unit.dtype))
        scratch += [sems((2, stages)), sems((2, stages))]
        operands.append(unit)
    outs = pl.pallas_call(
        partial(
            window_kernel, pays=pays, units=int(units), team=team, chunks=chunks, halo=halo,
            orders=orders,
        ),
        in_specs=[pl.BlockSpec(memory_space=pl.ANY)] * len(operands),
        out_specs=[pl.BlockSpec(memory_space=pl.ANY)] * len(shapes),
        out_shape=shapes,
        scratch_shapes=scratch,
        compiler_params=pltpu.CompilerParams(collective_id=collective_id, has_side_effects=True),
        name=name,
    )(*operands)
    if not units:
        return outs
    halves = []
    for color, order in enumerate(orders):
        held = outs[-1][color].reshape((2,) * stages + unit.shape[1:])
        dims = []
        for axis, size in (("rows", rows), ("seq", seq)):
            dims += [stages - 1 - order.index((axis, b)) for b in reversed(range(bits_of(size)))]
        held = held.transpose(dims + [stages, stages + 1])
        halves.append(held.reshape((rows, seq) + unit.shape[1:]))
    return outs[:-1], jnp.concatenate(halves, axis=2)


def pad_heads(value, axis, heads):
    groups = -(-heads // GROUP)
    shape = value.shape
    width = shape[axis] // heads
    value = value.reshape(shape[:axis] + (heads, width) + shape[axis + 1 :])
    pads = [(0, 0)] * value.ndim
    pads[axis] = (0, groups * GROUP - heads)
    value = jnp.pad(value, pads)
    value = value.reshape(shape[:axis] + (groups, GROUP * width) + shape[axis + 1 :])
    pads = [(0, 0)] * value.ndim
    pads[axis + 1] = (0, LANES - GROUP * width)
    value = jnp.pad(value, pads)
    return value.reshape(shape[:axis] + (groups * LANES,) + shape[axis + 1 :])


def drop_pad(value, axis, heads, width):
    groups = -(-heads // GROUP)
    shape = value.shape
    value = value.reshape(shape[:axis] + (groups, LANES) + shape[axis + 1 :])
    value = lax.slice_in_dim(value, 0, GROUP * width, axis=axis + 1)
    value = value.reshape(shape[:axis] + (groups * GROUP * width,) + shape[axis + 1 :])
    return lax.slice_in_dim(value, 0, heads * width, axis=axis)


def dot(a, b):
    return jnp.dot(a, b, preferred_element_type=F32)


def dot_nt(a, b):
    return lax.dot_general(a, b, (((1,), (1,)), ((), ())), preferred_element_type=F32)


def dot_tn(a, b):
    return lax.dot_general(a, b, (((0,), (0,)), ((), ())), preferred_element_type=F32)


def qkv_kernel(
    tok_ref, segc_ref, segr_ref, gain_ref, bias_ref, wrow_ref, brow_ref, wcol_ref,
    bcol_ref, krow_ref, vrow_ref, qrow_ref, kt_ref, vt_ref, qt_ref, *, scale,
):
    wide = krow_ref.shape[-1]
    width = kt_ref.shape[-2]
    x = tok_ref[0, 0].astype(F32)
    centre = jnp.mean(x, axis=-1, keepdims=True)
    x = x - centre
    inverse = lax.rsqrt(jnp.mean(x * x, axis=-1, keepdims=True) + NORM_EPS)
    normed = (x * inverse * gain_ref[...] + bias_ref[...]).astype(BF16)
    span = normed.shape[0]
    lane = lax.broadcasted_iota(jnp.int32, (span, wide), 1) % LANES
    kfeat = jnp.where(lane - FEATURE == segc_ref[0], 1.0, 0.0)
    rows = dot_nt(normed, wrow_ref[...]) + brow_ref[...]
    qrow_ref[0] = (rows[:, :wide] * scale).astype(BF16)
    krow_ref[0] = (rows[:, wide : 2 * wide] + kfeat).astype(BF16)
    vrow_ref[0] = rows[:, 2 * wide :].astype(BF16)
    cols = dot_nt(wcol_ref[...], normed) + bcol_ref[...]
    row = lax.broadcasted_iota(jnp.int32, (wide, span), 0) % LANES - FEATURE
    qfeat = jnp.where((row >= 0) & (row != segr_ref[0]), FAR, 0.0)
    qt_ref[0] = (cols[:wide] * scale + qfeat).astype(BF16)
    kt_ref[0] = cols[wide : wide + width].astype(BF16)
    vt_ref[0] = cols[wide + width :].astype(BF16)


def head_rows(h):
    row = lax.broadcasted_iota(jnp.int32, (LANES, TILE), 0)
    return (row // 32 == h % GROUP) | (row >= FEATURE)


def head_lanes(h):
    lane = lax.broadcasted_iota(jnp.int32, (TILE, LANES), 1)
    return (lane // 32 == h % GROUP) | (lane >= FEATURE)


def lanes_of(h):
    return slice((h // GROUP) * LANES, (h // GROUP + 1) * LANES)


def members_of(g, heads):
    return range(g * GROUP, min(heads, (g + 1) * GROUP))


def group_lanes(g):
    return slice(g * LANES, (g + 1) * LANES)


def spot_of(h):
    return slice((h % GROUP) * TILE, (h % GROUP + 1) * TILE)


def masked(keep, block):
    return jnp.where(keep, block, jnp.zeros_like(block))


def attend_kernel(
    first_ref, last_ref, krow_ref, vt_ref, qt_ref, out_ref, lse_ref, qpad, top, total, acc, *, heads
):
    row_at = pl.program_id(0)
    tiles = out_ref.shape[-1] // TILE
    groups = qpad.shape[0]
    stack = GROUP * TILE
    lse_ref[...] = jnp.zeros_like(lse_ref)
    qpad[...] = jnp.zeros_like(qpad)

    @pl.loop(0, tiles)
    def _(t):
        here = pl.ds(pl.multiple_of(t * TILE, TILE), TILE)
        for h in range(heads):
            qpad[h // GROUP, :, spot_of(h)] = masked(head_rows(h), qt_ref[0, lanes_of(h), here])
        top[...] = jnp.full_like(top, 2.0 * FAR)
        total[...] = jnp.zeros_like(total)
        acc[...] = jnp.zeros_like(acc)

        @pl.loop(first_ref[row_at, t], last_ref[row_at, t] + 1)
        def _(u):
            there = pl.ds(pl.multiple_of(u * TILE, TILE), TILE)
            def issue(g):
                depth = len(members_of(g, heads)) * TILE
                return dot(krow_ref[0, there, group_lanes(g)], qpad[g, :, :depth])

            ahead = issue(0)
            for g in range(groups):
                scores = ahead
                if g + 1 < groups:
                    ahead = issue(g + 1)
                depth = scores.shape[1]
                old = top[g : g + 1, :depth]
                new = jnp.maximum(old, jnp.max(scores, axis=0, keepdims=True))
                fade = jnp.exp2(old - new)
                probs = jnp.exp2(scores - new)
                top[g : g + 1, :depth] = new
                total[g : g + 1, :depth] = total[g : g + 1, :depth] * fade + jnp.sum(
                    probs, axis=0, keepdims=True
                )
                probs = probs.astype(BF16)
                for h in members_of(g, heads):
                    mine, spot = slice(h * 32, h * 32 + 32), spot_of(h)
                    acc[mine] = acc[mine] * fade[:, spot] + dot(vt_ref[0, mine, there], probs[:, spot])

        for h in range(heads):
            mine, g, spot = slice(h * 32, h * 32 + 32), h // GROUP, spot_of(h)
            out_ref[0, mine, here] = (acc[mine] / total[g : g + 1, spot]).astype(BF16)
            lse_ref[0, h : h + 1, here] = top[g : g + 1, spot] + jnp.log2(total[g : g + 1, spot])


def back_kernel(
    first_ref, last_ref, krow_ref, vrow_ref, qrow_ref, kt_ref, qt_ref, grow_ref, gt_ref, lse_ref,
    delta_ref, dqt_ref, dkrow_ref, dvrow_ref, qpad, gpad, qlanes, glanes, klanes, vlanes, stats,
    dk_acc, dv_acc, dq_acc, dk_far, dv_far, *, heads, start,
):
    row_at = pl.program_id(0)
    tiles = dqt_ref.shape[-1] // TILE
    groups = dk_acc.shape[-1] // LANES
    scale = 1.0 / math.sqrt(32.0)
    dk_acc[...] = jnp.zeros_like(dk_acc)
    dv_acc[...] = jnp.zeros_like(dv_acc)

    @pl.loop(0, tiles)
    def _(t):
        own = pl.ds(pl.multiple_of(t * TILE, TILE), TILE)
        here = pl.ds(pl.multiple_of((start + t) * TILE, TILE), TILE)
        first, last = first_ref[row_at, t], last_ref[row_at, t]
        for h in range(heads):
            g, spot = h // GROUP, spot_of(h)
            keep = head_rows(h)
            qpad[g, :, spot] = masked(keep, qt_ref[0, group_lanes(g), here])
            gpad[g, :, spot] = masked(keep, gt_ref[0, group_lanes(g), here])
            keep = head_lanes(h)
            qlanes[g, spot] = masked(keep, qrow_ref[0, here, group_lanes(g)])
            glanes[g, spot] = masked(keep, grow_ref[0, here, group_lanes(g)])
            stats[0, g : g + 1, spot] = lse_ref[0, h : h + 1, here]
            stats[1, g : g + 1, spot] = delta_ref[0, h : h + 1, here]
        dq_acc[...] = jnp.zeros_like(dq_acc)

        def issue(there, g):
            depth = len(members_of(g, heads)) * TILE
            scores = dot(krow_ref[0, there, group_lanes(g)], qpad[g, :, :depth])
            slope = dot(vrow_ref[0, there, group_lanes(g)], gpad[g, :, :depth])
            return scores, slope

        def pair(there, g, scores, slope):
            depth = scores.shape[1]
            probs = jnp.exp2(scores - stats[0, g : g + 1, :depth])
            ds = (probs * (slope - stats[1, g : g + 1, :depth])).astype(BF16)
            for h in members_of(g, heads):
                mine = slice(h * 32, h * 32 + 32)
                dq_acc[mine] += dot(kt_ref[0, mine, there], ds[:, spot_of(h)])
            return probs.astype(BF16), ds

        @pl.loop(jnp.maximum(first, start), jnp.minimum(last, start + tiles - 1) + 1)
        def _(u):
            there = pl.ds(pl.multiple_of(u * TILE, TILE), TILE)
            local = pl.ds(pl.multiple_of((u - start) * TILE, TILE), TILE)
            ahead = issue(there, 0)
            for g in range(groups):
                ready = ahead
                if g + 1 < groups:
                    ahead = issue(there, g + 1)
                probs, ds = pair(there, g, *ready)
                depth = probs.shape[1]
                dv_acc[local, group_lanes(g)] += dot(probs, glanes[g, :depth])
                dk_acc[local, group_lanes(g)] += dot(ds, qlanes[g, :depth])

        left = jnp.maximum(jnp.minimum(start, last + 1) - first, 0)
        beyond = jnp.maximum(start + tiles, first)
        right = jnp.maximum(last + 1 - beyond, 0)

        @pl.when(left + right > 0)
        def _():
            for h in range(heads):
                g, spot = h // GROUP, spot_of(h)
                keep = head_lanes(h)
                klanes[g, spot] = masked(keep, krow_ref[0, here, group_lanes(g)])
                vlanes[g, spot] = masked(keep, vrow_ref[0, here, group_lanes(g)])
            dk_far[...] = jnp.zeros_like(dk_far)
            dv_far[...] = jnp.zeros_like(dv_far)

            @pl.loop(0, left + right)
            def _(i):
                u = jnp.where(i < left, first + i, beyond + i - left)
                there = pl.ds(pl.multiple_of(u * TILE, TILE), TILE)

                def issue_far(g):
                    depth = len(members_of(g, heads)) * TILE
                    scores = dot(klanes[g, :depth], qt_ref[0, group_lanes(g), there])
                    return scores, dot(vlanes[g, :depth], gt_ref[0, group_lanes(g), there])

                ahead, ahead_far = issue(there, 0), issue_far(0)
                for g in range(groups):
                    ready, (scores, slope) = ahead, ahead_far
                    if g + 1 < groups:
                        ahead = issue(there, g + 1)
                    pair(there, g, *ready)
                    if g + 1 < groups:
                        ahead_far = issue_far(g + 1)
                    probs, ds = [], []
                    for h in members_of(g, heads):
                        spot = spot_of(h)
                        probs.append(jnp.exp2(scores[spot] - lse_ref[0, h : h + 1, there]))
                        ds.append(probs[-1] * (slope[spot] - delta_ref[0, h : h + 1, there]))
                    probs = jnp.concatenate([p.astype(BF16) for p in probs], axis=0)
                    ds = jnp.concatenate([d.astype(BF16) for d in ds], axis=0)
                    depth = probs.shape[0]
                    dv_far[g, :depth] += dot(probs, grow_ref[0, there, group_lanes(g)])
                    dk_far[g, :depth] += dot(ds, qrow_ref[0, there, group_lanes(g)])

            for g in range(groups):
                for acc, far in ((dv_acc, dv_far), (dk_acc, dk_far)):
                    added = acc[own, group_lanes(g)]
                    for h in members_of(g, heads):
                        added += masked(head_lanes(h), far[g, spot_of(h)])
                    acc[own, group_lanes(g)] = added

        dqt_ref[0, :, own] = (dq_acc[...] * scale).astype(BF16)

    dkrow_ref[0] = (dk_acc[...] * LN2).astype(BF16)
    dvrow_ref[0] = dv_acc[...].astype(BF16)


def feed_kernel(
    norm_ref, cot_ref, up_ref, down_ref, bias_ref, out_ref, back_ref, gup_ref, gdown_ref, gbias_ref,
    out_acc, back_acc, gup_acc, gdown_acc, gbias_acc, *, chunk,
):
    k, j = pl.program_id(0), pl.program_id(1)
    here = pl.ds(pl.multiple_of(j * chunk, chunk), chunk)
    norm, cot = norm_ref[0], cot_ref[0]
    up, down = up_ref[here, :], down_ref[here, :]
    pre = dot_nt(norm, up) + bias_ref[...]
    phi = 0.5 + 0.5 * lax.erf(pre * (1.0 / math.sqrt(2.0)))
    dens = jnp.exp(-0.5 * pre * pre) * (1.0 / math.sqrt(2.0 * math.pi))
    act = (pre * phi).astype(BF16)
    slope = dot_nt(cot, down) * (phi + pre * dens)
    slope_low = slope.astype(BF16)

    @pl.when(j == 0)
    def _():
        out_acc[...] = dot(act, down)
        back_acc[...] = dot(slope_low, up)

    @pl.when(j > 0)
    def _():
        out_acc[...] += dot(act, down)
        back_acc[...] += dot(slope_low, up)

    bias_sum = jnp.sum(slope_low.astype(F32), axis=0, keepdims=True)
    gup, gdown = dot_tn(slope_low, norm), dot_tn(act, cot)

    @pl.when(k == 0)
    def _():
        gup_acc[here, :] = gup
        gdown_acc[here, :] = gdown
        gbias_acc[pl.ds(j, 1)] = bias_sum

    @pl.when(k > 0)
    def _():
        gup_acc[here, :] += gup
        gdown_acc[here, :] += gdown
        gbias_acc[pl.ds(j, 1)] += bias_sum

    @pl.when(j == pl.num_programs(1) - 1)
    def _():
        out_ref[0] = out_acc[...].astype(BF16)
        back_ref[0] = back_acc[...].astype(BF16)

    @pl.when(k == pl.num_programs(0) - 1)
    def _():
        gup_ref[...] = gup_acc[here, :].astype(BF16)
        gdown_ref[...] = gdown_acc[here, :].astype(BF16)
        gbias_ref[0] = gbias_acc[pl.ds(j, 1)]


def norm_stats(value):
    centre = jnp.mean(value, axis=-1, keepdims=True)
    centred = value - centre
    inverse = lax.rsqrt(jnp.mean(centred * centred, axis=-1, keepdims=True) + NORM_EPS)
    return centred * inverse, inverse


def norm_back(upstream, unit_rows, inverse, gain):
    scaled = upstream * gain
    centred_mean = jnp.mean(scaled, axis=-1, keepdims=True)
    along_unit = jnp.mean(scaled * unit_rows, axis=-1, keepdims=True)
    return inverse * (scaled - centred_mean - unit_rows * along_unit)


def on_device(
    tokens, segments, ln1_gain, ln1_bias, w_qkv, q_bias, v_bias, w_out, out_bias, ln2_gain,
    ln2_bias, w_up, up_bias, w_down, down_bias, cotangent,
):
    nrow, span, model = tokens.shape
    rows, seq = lax.axis_size("rows"), lax.axis_size("seq")
    count = nrow * span
    width = model // HEADS
    ri, si = lax.axis_index("rows"), lax.axis_index("seq")
    grad_scale = 1.0 / math.sqrt(rows * nrow * seq * span)
    params = partial(pltpu.CompilerParams, vmem_limit_bytes=VMEM_LIMIT)

    team = max(g for g in (1, 2, 4) if HEADS % g == 0 and seq % g == 0 and g * span <= SEG_MOST)
    chunks, chunk = seq // team, team * span
    halo = -(-(SEG_MOST - 1) // chunk)
    blocks = (2 * halo + 1) * team
    window = blocks * span
    heads = HEADS // team
    here = heads * width
    groups = -(-heads // GROUP)
    wide = groups * LANES
    member = si % team

    def fetch(value_for, dc, k):
        perm = []
        for c in range(chunks):
            for m in range(team):
                if 0 <= c + dc < chunks:
                    perm.append(((c + dc) * team + (m + k) % team, c * team + m))
        value = value_for((member - k) % team)
        if dc == 0 and k == 0:
            return value
        return lax.ppermute(value, "seq", perm)

    def fetch_window(value_for):
        got = [fetch(value_for, dc, k) for dc in range(-halo, halo + 1) for k in range(team)]
        return jnp.stack(got)

    def in_order(rotated, axis):
        if team == 1:
            return rotated[0]
        twice = jnp.concatenate(list(rotated) * 2, axis=axis)
        size = rotated[0].shape[axis]
        return lax.dynamic_slice_in_dim(twice, ((team - member) % team) * size, team * size, axis)

    unit = 4 * model // (rows * seq)
    qkv_units = 3 * rows // 4
    shards = jnp.concatenate([w_qkv, w_out], axis=1).reshape(model // rows, rows, unit)
    shards = exchange(shards.transpose(1, 2, 0), "rows")
    shards = shards.transpose(1, 0, 2).reshape(2, unit // 2, model)
    windows = partial(window_of, team=team, chunks=chunks, halo=halo)
    (tok_win,), units = windows([tokens[None]], shards, 1, name="gather")
    qkv_t = units[:qkv_units].transpose(1, 0, 2, 3).reshape(3, team, here, model)
    out_t = units[qkv_units:].transpose(1, 0, 2, 3).reshape(model, model)
    seg_rot = fetch_window(lambda m: segments + 1)
    order = jnp.arange(blocks, dtype=jnp.int32)
    source = (order // team) * team + (order % team - member) % team
    segs = seg_rot[source].transpose(1, 0, 2).reshape(nrow, window)

    ff = up_bias.shape[0]
    hid = ff // rows
    part = ff // (rows * seq)
    both = jnp.stack([w_up.T, w_down])
    both = both.reshape(2, rows, part, model // rows)
    mine = exchange(both.transpose(1, 0, 2, 3), "rows")
    mine = mine.transpose(1, 2, 0, 3).reshape(2, part, model)
    feed_w = lax.all_gather(mine, "seq", axis=1, tiled=False).reshape(2, hid, model)
    my_up_bias = lax.dynamic_index_in_dim(
        up_bias.astype(F32).reshape(seq, rows, part), ri, 1, keepdims=False
    ).reshape(1, hid)

    cot_low = cotangent.reshape(count, model)
    cot_all = jnp.stack([swap(cot_low, "rows", k) if k else cot_low for k in range(rows)])

    gain_one, gain_two = ln1_gain.astype(F32)[None], ln2_gain.astype(F32)[None]
    shift_one, shift_two = ln1_bias.astype(F32)[None], ln2_bias.astype(F32)[None]
    my_w = lax.dynamic_index_in_dim(qkv_t, member, 1, keepdims=False)
    qb = lax.dynamic_index_in_dim(q_bias.astype(F32).reshape(team, here), member, 0, keepdims=False)
    vb = lax.dynamic_index_in_dim(v_bias.astype(F32).reshape(team, here), member, 0, keepdims=False)
    pad_w = [pad_heads(my_w[i], 0, heads) for i in range(3)]
    pad_qb, pad_vb = pad_heads(qb, 0, heads), pad_heads(vb, 0, heads)
    w_row = jnp.concatenate(pad_w, axis=0)
    b_row = jnp.concatenate([pad_qb, jnp.zeros_like(pad_qb), pad_vb])[None]
    w_col = jnp.concatenate([pad_w[0], my_w[1], my_w[2]], axis=0)
    b_col = jnp.concatenate([pad_qb, jnp.zeros_like(qb), vb])[:, None]

    whole = lambda *shape: pl.BlockSpec(shape, lambda *_: (0,) * len(shape))
    row_spec = pl.BlockSpec((1, span, wide), lambda r, b: (r, b, 0))
    col_spec = lambda size: pl.BlockSpec((1, size, span), lambda r, b: (r, 0, b))
    row_shape = jax.ShapeDtypeStruct((nrow, window, wide), BF16)
    col_shape = lambda size: jax.ShapeDtypeStruct((nrow, size, window), BF16)
    krow, vrow, qrow, kt, vt, qt = pl.pallas_call(
        partial(qkv_kernel, scale=LOG2E / math.sqrt(width)),
        grid_spec=pltpu.PrefetchScalarGridSpec(
            num_scalar_prefetch=0,
            grid=(nrow, blocks),
            in_specs=[
                pl.BlockSpec((1, 1, span, model), lambda r, b: (b, r, 0, 0)),
                pl.BlockSpec((1, span, 1), lambda r, b: (r, b, 0)),
                pl.BlockSpec((1, 1, span), lambda r, b: (r, 0, b)),
                whole(1, model), whole(1, model), whole(3 * wide, model), whole(1, 3 * wide),
                whole(wide + 2 * here, model), whole(wide + 2 * here, 1),
            ],
            out_specs=[row_spec] * 3 + [col_spec(here), col_spec(here), col_spec(wide)],
        ),
        out_shape=[row_shape] * 3 + [col_shape(here), col_shape(here), col_shape(wide)],
        compiler_params=params(),
        name="qkv",
    )(tok_win, segs[:, :, None], segs[:, None, :], gain_one, shift_one, w_row, b_row, w_col, b_col)

    tiles, start = chunk // TILE, halo * chunk // TILE
    own_segs = lax.slice_in_dim(segs, halo * chunk, (halo + 1) * chunk, axis=1)
    own_segs = own_segs.reshape(nrow, tiles, TILE)
    at = jnp.arange(window, dtype=jnp.int32)
    first = jnp.min(
        jnp.where(segs[:, None, :] == own_segs[:, :, :1], at, window), axis=-1
    ) // TILE
    last = jnp.max(jnp.where(segs[:, None, :] == own_segs[:, :, -1:], at, 0), axis=-1) // TILE

    once = pl.Buffered(1)
    per_row = lambda *shape: pl.BlockSpec(
        (1,) + shape, lambda r, *_: (r,) + (0,) * len(shape), pipeline_mode=once
    )
    stat = -(-heads // 8) * 8
    attended_t, lse = pl.pallas_call(
        partial(attend_kernel, heads=heads),
        grid_spec=pltpu.PrefetchScalarGridSpec(
            num_scalar_prefetch=2,
            grid=(nrow,),
            in_specs=[
                per_row(window, wide), per_row(here, window),
                pl.BlockSpec((1, wide, chunk), lambda r, *_: (r, 0, halo), pipeline_mode=once),
            ],
            out_specs=[per_row(here, chunk), per_row(stat, chunk)],
            scratch_shapes=[
                pltpu.VMEM((groups, LANES, GROUP * TILE), BF16),
                pltpu.VMEM((8, GROUP * TILE), F32), pltpu.VMEM((8, GROUP * TILE), F32),
                pltpu.VMEM((here, TILE), F32),
            ],
        ),
        out_shape=[
            jax.ShapeDtypeStruct((nrow, here, chunk), BF16),
            jax.ShapeDtypeStruct((nrow, stat, chunk), F32),
        ],
        compiler_params=params(),
        name="attend",
    )(first, last, krow, vt, qt)

    by_member = attended_t.reshape(nrow, here, team, span)
    joined = in_order(
        [
            fetch(lambda m: lax.dynamic_index_in_dim(by_member, m, 2, keepdims=False), 0, k)
            for k in range(team)
        ],
        1,
    )
    attended = joined.transpose(0, 2, 1).reshape(count, model)
    lse_parts = []
    for dc in range(-halo, halo + 1):
        if dc == 0:
            lse_parts.append(lse)
        else:
            perm = [
                ((c + dc) * team + m, c * team + m)
                for c in range(chunks) for m in range(team) if 0 <= c + dc < chunks
            ]
            lse_parts.append(lax.ppermute(lse, "seq", perm))
    lse_window = jnp.concatenate(lse_parts, axis=2)

    flat_tokens = tokens.reshape(count, model).astype(F32)
    residual = flat_tokens + dot_nt(attended, out_t) + out_bias.astype(F32)
    unit_two, inverse_two = norm_stats(residual)
    normed_two = (unit_two * gain_two + shift_two).astype(BF16)

    norm_all = jnp.stack([swap(normed_two, "rows", k) if k else normed_two for k in range(rows)])
    step = 256 if hid % 256 == 0 else LANES
    tok_spec = pl.BlockSpec((1, count, model), lambda k, j: (k, 0, 0))
    grad_spec = pl.BlockSpec((step, model), lambda k, j: (jnp.where(k == rows - 1, j, 0), 0))
    out_parts, back_parts, grad_up, grad_down, grad_up_bias = pl.pallas_call(
        partial(feed_kernel, chunk=step),
        grid=(rows, hid // step),
        in_specs=[
            tok_spec, tok_spec,
            whole(hid, model), whole(hid, model),
            pl.BlockSpec((1, step), lambda k, j: (0, j)),
        ],
        out_specs=[
            tok_spec, tok_spec, grad_spec, grad_spec,
            pl.BlockSpec((1, 1, step), lambda k, j: (jnp.where(k == rows - 1, j, 0), 0, 0)),
        ],
        out_shape=[
            jax.ShapeDtypeStruct((rows, count, model), BF16),
            jax.ShapeDtypeStruct((rows, count, model), BF16),
            jax.ShapeDtypeStruct((hid, model), BF16),
            jax.ShapeDtypeStruct((hid, model), BF16),
            jax.ShapeDtypeStruct((hid // step, 1, step), F32),
        ],
        scratch_shapes=[
            pltpu.VMEM((count, model), F32), pltpu.VMEM((count, model), F32),
            pltpu.VMEM((hid, model), F32), pltpu.VMEM((hid, model), F32),
            pltpu.VMEM((hid // step, step), F32),
        ],
        compiler_params=params(),
        name="feed",
    )(norm_all, cot_all, feed_w[0], feed_w[1], my_up_bias)

    normed_two_grad = back_parts[0].astype(F32)
    for k in range(1, rows):
        normed_two_grad = normed_two_grad + swap(back_parts[k], "rows", k).astype(F32)
    result = residual + down_bias.astype(F32) + out_parts[0].astype(F32)
    for k in range(1, rows):
        result = result + swap(out_parts[k], "rows", k).astype(F32)
    output = result.astype(BF16).reshape(tokens.shape)

    feed_grad = jnp.stack(
        [grad_up.reshape(seq, part, model), grad_down.reshape(seq, part, model)], axis=1
    )
    feed_sum = lax.psum_scatter(feed_grad, "seq", scatter_dimension=0, tiled=False)
    feed_sum = feed_sum.reshape(2, part, rows, model // rows)
    back = exchange(feed_sum.transpose(2, 0, 1, 3), "rows")
    back = back.transpose(1, 0, 2, 3).reshape(2, ff // seq, model // rows).astype(F32) * grad_scale
    sum_up, sum_down = back[0].T, back[1]

    cot_wide = cot_low.astype(F32)
    grad_gain_two = jnp.sum(normed_two_grad * unit_two, axis=0)
    grad_shift_two = jnp.sum(normed_two_grad, axis=0)
    residual_grad = cot_wide + norm_back(normed_two_grad, unit_two, inverse_two, gain_two)
    branch_grad = residual_grad.astype(BF16)
    grad_out_t = dot_tn(branch_grad, attended).astype(BF16)
    grad_out_bias = jnp.sum(branch_grad, axis=0, dtype=F32)
    attended_grad = dot(branch_grad, out_t).astype(BF16)

    wide_bias = jnp.zeros((seq, rows, part), F32)
    wide_bias = lax.dynamic_update_index_in_dim(
        wide_bias, grad_up_bias.reshape(seq, part), ri, 1
    ).reshape(ff)
    early = [
        grad_out_bias, grad_gain_two, grad_shift_two, jnp.sum(cot_low, axis=0, dtype=F32), wide_bias,
    ]

    delta = jnp.sum(
        (attended.astype(F32) * attended_grad.astype(F32)).reshape(nrow, span, HEADS, width), axis=-1
    ).transpose(0, 2, 1)
    delta = jnp.pad(delta.reshape(nrow, team, heads, span), ((0, 0), (0, 0), (0, stat - heads), (0, 0)))
    grad_members = attended_grad.reshape(nrow, span, team, here)
    grad_win, delta_win = windows(
        [grad_members.transpose(2, 0, 1, 3), delta.transpose(1, 0, 2, 3)], None, 2, name="grads"
    )
    grad_win = grad_win.transpose(1, 0, 2, 3).reshape(nrow, window, here)
    delta_win = delta_win.transpose(1, 2, 0, 3).reshape(nrow, stat, window)
    grow = pad_heads(grad_win, 2, heads)
    gt = grow.transpose(0, 2, 1)

    dqt, dkrow, dvrow = pl.pallas_call(
        partial(back_kernel, heads=heads, start=start),
        grid_spec=pltpu.PrefetchScalarGridSpec(
            num_scalar_prefetch=2,
            grid=(nrow,),
            in_specs=[
                per_row(window, wide), per_row(window, wide), per_row(window, wide),
                per_row(here, window), per_row(wide, window), per_row(window, wide),
                per_row(wide, window), per_row(stat, window), per_row(stat, window),
            ],
            out_specs=[per_row(here, chunk), per_row(chunk, wide), per_row(chunk, wide)],
            scratch_shapes=[
                *[pltpu.VMEM((groups, LANES, GROUP * TILE), BF16)] * 2,
                *[pltpu.VMEM((groups, GROUP * TILE, LANES), BF16)] * 4,
                pltpu.VMEM((2, 8, GROUP * TILE), F32),
                pltpu.VMEM((chunk, wide), F32), pltpu.VMEM((chunk, wide), F32),
                pltpu.VMEM((here, TILE), F32),
                *[pltpu.VMEM((groups, GROUP * TILE, LANES), F32)] * 2,
            ],
        ),
        out_shape=[
            jax.ShapeDtypeStruct((nrow, here, chunk), BF16),
            jax.ShapeDtypeStruct((nrow, chunk, wide), BF16),
            jax.ShapeDtypeStruct((nrow, chunk, wide), BF16),
        ],
        compiler_params=params(),
        name="attend_back",
    )(first, last, krow, vrow, qrow, kt, qt, grow, gt, lse_window, delta_win)

    mixed = jnp.concatenate(
        [dqt.transpose(0, 2, 1), drop_pad(dkrow, 2, heads, width), drop_pad(dvrow, 2, heads, width)],
        axis=2,
    )
    mixed_flat = mixed.reshape(nrow * chunk, 3 * here)
    chunk_tokens = tok_win[halo * team : (halo + 1) * team].transpose(1, 0, 2, 3)
    chunk_unit, _ = norm_stats(chunk_tokens.astype(F32).reshape(nrow * chunk, model))
    chunk_norm = (chunk_unit * gain_one + shift_one).astype(BF16)
    grad_qkv_t = dot_tn(mixed_flat, chunk_norm).astype(BF16)
    bias_sums = jnp.sum(mixed_flat, axis=0, dtype=F32).reshape(3, here)
    back_part = dot(mixed_flat, my_w.reshape(3 * here, model)).astype(BF16)
    back_members = back_part.reshape(nrow, team, span, model)
    normed_one_grad = 0.0
    for k in range(team):
        normed_one_grad = normed_one_grad + fetch(
            lambda m: lax.dynamic_index_in_dim(back_members, m, 1, keepdims=False), 0, k
        ).astype(F32)
    normed_one_grad = normed_one_grad.reshape(count, model)
    unit_one, inverse_one = norm_stats(flat_tokens)
    grad_gain_one = jnp.sum(normed_one_grad * unit_one, axis=0)
    grad_shift_one = jnp.sum(normed_one_grad, axis=0)
    tokens_grad = residual_grad + norm_back(normed_one_grad, unit_one, inverse_one, gain_one)
    tokens_grad = tokens_grad.astype(BF16).reshape(tokens.shape)

    at_member = (jnp.arange(team) == member)[None, :, None, None]
    spread = jnp.where(at_member, grad_qkv_t.reshape(3, 1, here, model), jnp.zeros((), BF16))
    spread = spread.reshape(seq, qkv_units, unit, model)
    spread = jnp.concatenate([spread, grad_out_t.reshape(seq, rows - qkv_units, unit, model)], axis=1)
    sums = scatter_sum(spread.transpose(1, 0, 2, 3))
    sums = exchange(sums.reshape(unit, rows, model // rows).transpose(1, 0, 2), "rows")
    sums = sums.reshape(rows * unit, model // rows).T.astype(F32) * grad_scale
    sum_qkv, sum_out = sums[:, : qkv_units * unit], sums[:, qkv_units * unit :]

    bias_full = jnp.where(at_member[:, :, 0], bias_sums[0::2][:, None], 0.0)
    flat = sum_all(
        jnp.concatenate([*early, grad_gain_one, grad_shift_one, bias_full.reshape(2 * model)])
    ) * grad_scale
    sum_out_bias, sum_gain_two, sum_shift_two, sum_down_bias = (
        flat[i * model : (i + 1) * model] for i in range(4)
    )
    sum_up_bias = flat[4 * model : 4 * model + ff]
    sum_gain_one, sum_shift_one, sum_q_bias, sum_v_bias = (
        flat[4 * model + ff + i * model : 4 * model + ff + (i + 1) * model] for i in range(4)
    )

    return (
        output, tokens_grad, sum_gain_one, sum_shift_one, sum_qkv, sum_q_bias, sum_v_bias, sum_out,
        sum_out_bias, sum_gain_two, sum_shift_two, sum_up, sum_up_bias, sum_down, sum_down_bias,
    )


def solution(mesh):
    tok, mat, rep = P("rows", "seq", None), P("rows", "seq"), P()
    in_specs = (
        tok, mat, rep, rep, mat, rep, rep, mat, rep, rep, rep, mat, rep, P("seq", "rows"), rep, tok,
    )
    out_specs = (
        tok, tok, rep, rep, mat, rep, rep, mat, rep, rep, rep, mat, rep, P("seq", "rows"), rep,
    )
    return jax.shard_map(
        on_device, mesh=mesh, in_specs=in_specs, out_specs=out_specs, check_vma=False
    )
```

```python
import math
from functools import partial

import jax
import jax.numpy as jnp
from jax import lax
from jax.experimental import pallas as pl
from jax.experimental.pallas import tpu as pltpu
from jax.sharding import PartitionSpec as P

HEADS = 20
SEG_MOST = 1024
NORM_EPS = 1e-05
F32 = jnp.float32
BF16 = jnp.bfloat16
LOG2E = 1.4426950408889634
LN2 = 0.6931471805599453
FAR = -1e30
LANES = 128
TILE = 128
GROUP = 3
FEATURE = 96
VMEM_LIMIT = 60 * 1024 * 1024


def bits_of(size):
    return size.bit_length() - 1


def swap(value, axis, mask):
    size = lax.axis_size(axis)
    return lax.ppermute(value, axis, [(i, i ^ mask) for i in range(size)])


def exchange(pieces, axis):
    size, me = lax.axis_size(axis), lax.axis_index(axis)
    out = pieces
    for k in range(1, size):
        got = swap(lax.dynamic_index_in_dim(pieces, me ^ k, 0, keepdims=False), axis, k)
        out = lax.dynamic_update_index_in_dim(out, got, me ^ k, 0)
    return out


def gather_all(block):
    rows, seq = lax.axis_size("rows"), lax.axis_size("seq")
    stages = [("seq", b) for b in reversed(range(bits_of(seq)))]
    stages += [("rows", b) for b in reversed(range(bits_of(rows)))]
    place = 0
    for weight, (axis, bit) in enumerate(stages):
        place = place + (((lax.axis_index(axis) >> bit) & 1) << weight)
    total = rows * seq
    held = jnp.zeros((total,) + block.shape, block.dtype)
    held = lax.dynamic_update_index_in_dim(held, block, place, 0)
    for weight, (axis, bit) in enumerate(stages):
        width = 1 << weight
        mine = (place >> weight) << weight
        other = mine ^ width
        got = swap(lax.dynamic_slice_in_dim(held, mine, width, 0), axis, 1 << bit)
        held = lax.dynamic_update_slice_in_dim(held, got, other, 0)
    count = len(stages)
    held = held.reshape((2,) * count + block.shape)
    dims = []
    for axis, size in (("rows", rows), ("seq", seq)):
        for b in reversed(range(bits_of(size))):
            dims.append(count - 1 - stages.index((axis, b)))
    dims += list(range(count, count + block.ndim))
    return held.transpose(dims).reshape((rows, seq) + block.shape)


def scatter_sum(parts):
    rows, seq = lax.axis_size("rows"), lax.axis_size("seq")
    rb, sb = bits_of(rows), bits_of(seq)
    tail = parts.shape[2:]
    parts = parts.reshape((2,) * (rb + sb) + tail)
    dims = list(reversed(range(rb))) + [rb + d for d in reversed(range(sb))]
    dims += list(range(rb + sb, rb + sb + len(tail)))
    parts = parts.transpose(dims)
    for axis, count in (("rows", rb), ("seq", sb)):
        for b in range(count):
            bit = (lax.axis_index(axis) >> b) & 1
            keep = lax.dynamic_index_in_dim(parts, bit, 0, keepdims=False)
            send = lax.dynamic_index_in_dim(parts, 1 - bit, 0, keepdims=False)
            got = swap(send, axis, 1 << b)
            parts = (keep.astype(F32) + got.astype(F32)).astype(BF16)
    return parts


def sum_all(value):
    for axis in ("rows", "seq"):
        for b in range(bits_of(lax.axis_size(axis))):
            value = value + swap(value, axis, 1 << b)
    return value


def gather_orders(rows, seq):
    seq_bits = [("seq", b) for b in reversed(range(bits_of(seq)))]
    row_bits = [("rows", b) for b in reversed(range(bits_of(rows)))]
    return seq_bits + row_bits, row_bits[:-1] + seq_bits + row_bits[-1:]


def bit_at(value, bit):
    return value // (1 << bit) % 2


def flipped(value, bit):
    return value + (1 - 2 * bit_at(value, bit)) * (1 << bit)


def window_kernel(*refs, pays, units, team, chunks, halo, orders):
    total = pays + units
    ins, outs = refs[:total], refs[total : 2 * total]
    keep_sem, mate_send, mate_recv, far_send, far_recv = refs[2 * total : 2 * total + 5]
    rows, seq = lax.axis_size("rows"), lax.axis_size("seq")
    r, s = lax.axis_index("rows"), lax.axis_index("seq")
    c, m = s // team, s % team

    barrier = pltpu.get_barrier_semaphore()
    for j in range(1, seq):
        pl.semaphore_signal(barrier, inc=1, device_id={"seq": (s + j) % seq})
    if units:
        for j in range(1, rows):
            pl.semaphore_signal(barrier, inc=1, device_id={"rows": (r + j) % rows})
    pl.semaphore_wait(barrier, seq - 1 + (rows - 1) * units)

    def piece(p, member):
        return ins[p].at[member] if ins[p].shape[0] > 1 else ins[p].at[0]

    def mate(p, k):
        to = (m + k) % team
        return pltpu.make_async_remote_copy(
            src_ref=piece(p, to), dst_ref=outs[p].at[halo * team + m],
            send_sem=mate_send.at[p, k], recv_sem=mate_recv.at[p, k], device_id={"seq": c * team + to},
        )

    def mate_got(p, k):
        slot = outs[p].at[halo * team + (m + team - k) % team]
        return pltpu.make_async_remote_copy(
            src_ref=slot, dst_ref=slot, send_sem=mate_send.at[p, k], recv_sem=mate_recv.at[p, k],
            device_id={"seq": c * team + (m + k) % team},
        )

    steps = [d for n in range(1, halo + 1) for d in (-n, n)]

    def far(p, i, k):
        d, mm = steps[i], (m + team - k) % team
        src = piece(p, m) if k == 0 else outs[p].at[halo * team + mm]
        return pltpu.make_async_remote_copy(
            src_ref=src, dst_ref=outs[p].at[(halo - d) * team + mm],
            send_sem=far_send.at[p, i, k], recv_sem=far_recv.at[p, i, k],
            device_id={"seq": (c + d) * team + m},
        )

    def far_got(p, i, k):
        slot = outs[p].at[(halo - steps[i]) * team + (m + team - k) % team]
        return pltpu.make_async_remote_copy(
            src_ref=slot, dst_ref=slot, send_sem=far_send.at[p, i, k], recv_sem=far_recv.at[p, i, k],
            device_id={"seq": (c + steps[i]) * team + m},
        )

    def sends(i):
        return (c + steps[i] >= 0) & (c + steps[i] < chunks)

    def gets(i):
        return (c - steps[i] >= 0) & (c - steps[i] < chunks)

    def start_far(k):
        for i in range(len(steps)):
            @pl.when(sends(i))
            def _():
                for p in range(pays):
                    far(p, i, k).start()

    keeps = [
        pltpu.make_async_copy(piece(p, m), outs[p].at[halo * team + m], keep_sem.at[p])
        for p in range(pays)
    ]
    if units:
        unit_send, unit_recv = refs[2 * total + 5 :]
        unit_ref, unit_out = ins[-1], outs[-1]
        places = []
        for order in orders:
            place = 0
            for n, (axis, bit) in enumerate(order):
                place = place + bit_at(r if axis == "rows" else s, bit) * (1 << n)
            places.append(place)
            keeps.append(
                pltpu.make_async_copy(
                    unit_ref.at[len(places) - 1], unit_out.at[len(places) - 1, place],
                    keep_sem.at[pays + len(places) - 1],
                )
            )

        def stage(color, n):
            axis, bit = orders[color][n]
            width = 1 << n
            mine = places[color] // width * width
            group = unit_out.at[color, pl.ds(mine, width)]
            return pltpu.make_async_remote_copy(
                src_ref=group, dst_ref=group, send_sem=unit_send.at[color, n],
                recv_sem=unit_recv.at[color, n], device_id={axis: flipped(r if axis == "rows" else s, bit)},
            )

        def stage_got(color, n):
            axis, bit = orders[color][n]
            width = 1 << n
            group = unit_out.at[color, pl.ds(flipped(places[color] // width, 0) * width, width)]
            return pltpu.make_async_remote_copy(
                src_ref=group, dst_ref=group, send_sem=unit_send.at[color, n],
                recv_sem=unit_recv.at[color, n], device_id={axis: flipped(r if axis == "rows" else s, bit)},
            )

    for copy in keeps:
        copy.start()
    for k in range(1, team):
        for p in range(pays):
            mate(p, k).start()
    start_far(0)
    forwards = list(range(1, team))

    def forward():
        k = forwards.pop(0)
        for p in range(pays):
            mate_got(p, k).wait_recv()
        start_far(k)

    if units:
        for color in range(2):
            keeps[pays + color].wait()
            stage(color, 0).start()
        for n in range(1, len(orders[0])):
            for color in range(2):
                stage_got(color, n - 1).wait_recv()
                stage(color, n).start()
            if n >= 2 and forwards:
                forward()
    while forwards:
        forward()
    for p in range(pays):
        keeps[p].wait()
    for k in range(1, team):
        for p in range(pays):
            mate(p, k).wait_send()
    for i in range(len(steps)):
        for k in range(team):
            @pl.when(gets(i))
            def _():
                for p in range(pays):
                    far_got(p, i, k).wait_recv()

            @pl.when(sends(i))
            def _():
                for p in range(pays):
                    far(p, i, k).wait_send()
    if units:
        final = len(orders[0]) - 1
        for color in range(2):
            stage_got(color, final).wait_recv()
            for n in range(final + 1):
                stage(color, n).wait_send()


def window_of(payloads, unit, collective_id, *, team, chunks, halo, name):
    rows, seq = lax.axis_size("rows"), lax.axis_size("seq")
    orders = gather_orders(rows, seq)
    units = unit is not None
    blocks = (2 * halo + 1) * team
    shapes = [jax.ShapeDtypeStruct((blocks,) + p.shape[1:], p.dtype) for p in payloads]
    pays, steps, stages = len(payloads), 2 * halo, len(orders[0])
    sems = pltpu.SemaphoreType.DMA
    scratch = [
        sems((pays + 2,)), sems((pays, team)), sems((pays, team)), sems((pays, steps, team)),
        sems((pays, steps, team)),
    ]
    operands = list(payloads)
    if units:
        shapes.append(jax.ShapeDtypeStruct((2, rows * seq) + unit.shape[1:], unit.dtype))
        scratch += [sems((2, stages)), sems((2, stages))]
        operands.append(unit)
    outs = pl.pallas_call(
        partial(
            window_kernel, pays=pays, units=int(units), team=team, chunks=chunks, halo=halo,
            orders=orders,
        ),
        in_specs=[pl.BlockSpec(memory_space=pl.ANY)] * len(operands),
        out_specs=[pl.BlockSpec(memory_space=pl.ANY)] * len(shapes),
        out_shape=shapes,
        scratch_shapes=scratch,
        compiler_params=pltpu.CompilerParams(collective_id=collective_id, has_side_effects=True),
        name=name,
    )(*operands)
    if not units:
        return outs
    halves = []
    for color, order in enumerate(orders):
        held = outs[-1][color].reshape((2,) * stages + unit.shape[1:])
        dims = []
        for axis, size in (("rows", rows), ("seq", seq)):
            dims += [stages - 1 - order.index((axis, b)) for b in reversed(range(bits_of(size)))]
        held = held.transpose(dims + [stages, stages + 1])
        halves.append(held.reshape((rows, seq) + unit.shape[1:]))
    return outs[:-1], jnp.concatenate(halves, axis=2)


def pad_heads(value, axis, heads):
    groups = -(-heads // GROUP)
    shape = value.shape
    width = shape[axis] // heads
    value = value.reshape(shape[:axis] + (heads, width) + shape[axis + 1 :])
    pads = [(0, 0)] * value.ndim
    pads[axis] = (0, groups * GROUP - heads)
    value = jnp.pad(value, pads)
    value = value.reshape(shape[:axis] + (groups, GROUP * width) + shape[axis + 1 :])
    pads = [(0, 0)] * value.ndim
    pads[axis + 1] = (0, LANES - GROUP * width)
    value = jnp.pad(value, pads)
    return value.reshape(shape[:axis] + (groups * LANES,) + shape[axis + 1 :])


def drop_pad(value, axis, heads, width):
    groups = -(-heads // GROUP)
    shape = value.shape
    value = value.reshape(shape[:axis] + (groups, LANES) + shape[axis + 1 :])
    value = lax.slice_in_dim(value, 0, GROUP * width, axis=axis + 1)
    value = value.reshape(shape[:axis] + (groups * GROUP * width,) + shape[axis + 1 :])
    return lax.slice_in_dim(value, 0, heads * width, axis=axis)


def dot(a, b):
    return jnp.dot(a, b, preferred_element_type=F32)


def dot_nt(a, b):
    return lax.dot_general(a, b, (((1,), (1,)), ((), ())), preferred_element_type=F32)


def dot_tn(a, b):
    return lax.dot_general(a, b, (((0,), (0,)), ((), ())), preferred_element_type=F32)


def qkv_kernel(
    tok_ref, segc_ref, segr_ref, gain_ref, bias_ref, wrow_ref, brow_ref, wcol_ref,
    bcol_ref, krow_ref, vrow_ref, qrow_ref, kt_ref, vt_ref, qt_ref, *, scale,
):
    wide = krow_ref.shape[-1]
    width = kt_ref.shape[-2]
    x = tok_ref[0, 0].astype(F32)
    centre = jnp.mean(x, axis=-1, keepdims=True)
    x = x - centre
    inverse = lax.rsqrt(jnp.mean(x * x, axis=-1, keepdims=True) + NORM_EPS)
    normed = (x * inverse * gain_ref[...] + bias_ref[...]).astype(BF16)
    span = normed.shape[0]
    lane = lax.broadcasted_iota(jnp.int32, (span, wide), 1) % LANES
    kfeat = jnp.where(lane - FEATURE == segc_ref[0], 1.0, 0.0)
    rows = dot_nt(normed, wrow_ref[...]) + brow_ref[...]
    qrow_ref[0] = (rows[:, :wide] * scale).astype(BF16)
    krow_ref[0] = (rows[:, wide : 2 * wide] + kfeat).astype(BF16)
    vrow_ref[0] = rows[:, 2 * wide :].astype(BF16)
    cols = dot_nt(wcol_ref[...], normed) + bcol_ref[...]
    row = lax.broadcasted_iota(jnp.int32, (wide, span), 0) % LANES - FEATURE
    qfeat = jnp.where((row >= 0) & (row != segr_ref[0]), FAR, 0.0)
    qt_ref[0] = (cols[:wide] * scale + qfeat).astype(BF16)
    kt_ref[0] = cols[wide : wide + width].astype(BF16)
    vt_ref[0] = cols[wide + width :].astype(BF16)


def head_rows(h):
    row = lax.broadcasted_iota(jnp.int32, (LANES, TILE), 0)
    return (row // 32 == h % GROUP) | (row >= FEATURE)


def head_lanes(h):
    lane = lax.broadcasted_iota(jnp.int32, (TILE, LANES), 1)
    return (lane // 32 == h % GROUP) | (lane >= FEATURE)


def lanes_of(h):
    return slice((h // GROUP) * LANES, (h // GROUP + 1) * LANES)


def members_of(g, heads):
    return range(g * GROUP, min(heads, (g + 1) * GROUP))


def group_lanes(g):
    return slice(g * LANES, (g + 1) * LANES)


def spot_of(h):
    return slice((h % GROUP) * TILE, (h % GROUP + 1) * TILE)


def masked(keep, block):
    return jnp.where(keep, block, jnp.zeros_like(block))


def attend_kernel(
    first_ref, last_ref, krow_ref, vt_ref, qt_ref, out_ref, lse_ref, qpad, top, total, acc, *, heads
):
    row_at = pl.program_id(0)
    tiles = out_ref.shape[-1] // TILE
    groups = qpad.shape[0]
    stack = GROUP * TILE
    lse_ref[...] = jnp.zeros_like(lse_ref)
    qpad[...] = jnp.zeros_like(qpad)

    @pl.loop(0, tiles)
    def _(t):
        here = pl.ds(pl.multiple_of(t * TILE, TILE), TILE)
        for h in range(heads):
            qpad[h // GROUP, :, spot_of(h)] = masked(head_rows(h), qt_ref[0, lanes_of(h), here])
        top[...] = jnp.full_like(top, 2.0 * FAR)
        total[...] = jnp.zeros_like(total)
        acc[...] = jnp.zeros_like(acc)

        @pl.loop(first_ref[row_at, t], last_ref[row_at, t] + 1)
        def _(u):
            there = pl.ds(pl.multiple_of(u * TILE, TILE), TILE)
            def issue(g):
                depth = len(members_of(g, heads)) * TILE
                return dot(krow_ref[0, there, group_lanes(g)], qpad[g, :, :depth])

            ahead = issue(0)
            for g in range(groups):
                scores = ahead
                if g + 1 < groups:
                    ahead = issue(g + 1)
                depth = scores.shape[1]
                old = top[g : g + 1, :depth]
                new = jnp.maximum(old, jnp.max(scores, axis=0, keepdims=True))
                fade = jnp.exp2(old - new)
                probs = jnp.exp2(scores - new)
                top[g : g + 1, :depth] = new
                total[g : g + 1, :depth] = total[g : g + 1, :depth] * fade + jnp.sum(
                    probs, axis=0, keepdims=True
                )
                probs = probs.astype(BF16)
                for h in members_of(g, heads):
                    mine, spot = slice(h * 32, h * 32 + 32), spot_of(h)
                    acc[mine] = acc[mine] * fade[:, spot] + dot(vt_ref[0, mine, there], probs[:, spot])

        for h in range(heads):
            mine, g, spot = slice(h * 32, h * 32 + 32), h // GROUP, spot_of(h)
            out_ref[0, mine, here] = (acc[mine] / total[g : g + 1, spot]).astype(BF16)
            lse_ref[0, h : h + 1, here] = top[g : g + 1, spot] + jnp.log2(total[g : g + 1, spot])


def back_kernel(
    first_ref, last_ref, krow_ref, vrow_ref, qrow_ref, kt_ref, qt_ref, grow_ref, gt_ref, lse_ref,
    delta_ref, dqt_ref, dkrow_ref, dvrow_ref, qpad, gpad, qlanes, glanes, klanes, vlanes, stats,
    dk_acc, dv_acc, dq_acc, dk_far, dv_far, *, heads, start,
):
    row_at = pl.program_id(0)
    tiles = dqt_ref.shape[-1] // TILE
    groups = dk_acc.shape[-1] // LANES
    scale = 1.0 / math.sqrt(32.0)
    dk_acc[...] = jnp.zeros_like(dk_acc)
    dv_acc[...] = jnp.zeros_like(dv_acc)

    @pl.loop(0, tiles)
    def _(t):
        own = pl.ds(pl.multiple_of(t * TILE, TILE), TILE)
        here = pl.ds(pl.multiple_of((start + t) * TILE, TILE), TILE)
        first, last = first_ref[row_at, t], last_ref[row_at, t]
        for h in range(heads):
            g, spot = h // GROUP, spot_of(h)
            keep = head_rows(h)
            qpad[g, :, spot] = masked(keep, qt_ref[0, group_lanes(g), here])
            gpad[g, :, spot] = masked(keep, gt_ref[0, group_lanes(g), here])
            keep = head_lanes(h)
            qlanes[g, spot] = masked(keep, qrow_ref[0, here, group_lanes(g)])
            glanes[g, spot] = masked(keep, grow_ref[0, here, group_lanes(g)])
            stats[0, g : g + 1, spot] = lse_ref[0, h : h + 1, here]
            stats[1, g : g + 1, spot] = delta_ref[0, h : h + 1, here]
        dq_acc[...] = jnp.zeros_like(dq_acc)

        def issue(there, g):
            depth = len(members_of(g, heads)) * TILE
            scores = dot(krow_ref[0, there, group_lanes(g)], qpad[g, :, :depth])
            slope = dot(vrow_ref[0, there, group_lanes(g)], gpad[g, :, :depth])
            return scores, slope

        def pair(there, g, scores, slope):
            depth = scores.shape[1]
            probs = jnp.exp2(scores - stats[0, g : g + 1, :depth])
            ds = (probs * (slope - stats[1, g : g + 1, :depth])).astype(BF16)
            for h in members_of(g, heads):
                mine = slice(h * 32, h * 32 + 32)
                dq_acc[mine] += dot(kt_ref[0, mine, there], ds[:, spot_of(h)])
            return probs.astype(BF16), ds

        @pl.loop(jnp.maximum(first, start), jnp.minimum(last, start + tiles - 1) + 1)
        def _(u):
            there = pl.ds(pl.multiple_of(u * TILE, TILE), TILE)
            local = pl.ds(pl.multiple_of((u - start) * TILE, TILE), TILE)
            ahead = issue(there, 0)
            for g in range(groups):
                ready = ahead
                if g + 1 < groups:
                    ahead = issue(there, g + 1)
                probs, ds = pair(there, g, *ready)
                depth = probs.shape[1]
                dv_acc[local, group_lanes(g)] += dot(probs, glanes[g, :depth])
                dk_acc[local, group_lanes(g)] += dot(ds, qlanes[g, :depth])

        left = jnp.maximum(jnp.minimum(start, last + 1) - first, 0)
        beyond = jnp.maximum(start + tiles, first)
        right = jnp.maximum(last + 1 - beyond, 0)

        @pl.when(left + right > 0)
        def _():
            for h in range(heads):
                g, spot = h // GROUP, spot_of(h)
                keep = head_lanes(h)
                klanes[g, spot] = masked(keep, krow_ref[0, here, group_lanes(g)])
                vlanes[g, spot] = masked(keep, vrow_ref[0, here, group_lanes(g)])
            dk_far[...] = jnp.zeros_like(dk_far)
            dv_far[...] = jnp.zeros_like(dv_far)

            @pl.loop(0, left + right)
            def _(i):
                u = jnp.where(i < left, first + i, beyond + i - left)
                there = pl.ds(pl.multiple_of(u * TILE, TILE), TILE)

                def issue_far(g):
                    depth = len(members_of(g, heads)) * TILE
                    scores = dot(klanes[g, :depth], qt_ref[0, group_lanes(g), there])
                    return scores, dot(vlanes[g, :depth], gt_ref[0, group_lanes(g), there])

                ahead, ahead_far = issue(there, 0), issue_far(0)
                for g in range(groups):
                    ready, (scores, slope) = ahead, ahead_far
                    if g + 1 < groups:
                        ahead = issue(there, g + 1)
                    pair(there, g, *ready)
                    if g + 1 < groups:
                        ahead_far = issue_far(g + 1)
                    probs, ds = [], []
                    for h in members_of(g, heads):
                        spot = spot_of(h)
                        probs.append(jnp.exp2(scores[spot] - lse_ref[0, h : h + 1, there]))
                        ds.append(probs[-1] * (slope[spot] - delta_ref[0, h : h + 1, there]))
                    probs = jnp.concatenate([p.astype(BF16) for p in probs], axis=0)
                    ds = jnp.concatenate([d.astype(BF16) for d in ds], axis=0)
                    depth = probs.shape[0]
                    dv_far[g, :depth] += dot(probs, grow_ref[0, there, group_lanes(g)])
                    dk_far[g, :depth] += dot(ds, qrow_ref[0, there, group_lanes(g)])

            for g in range(groups):
                for acc, far in ((dv_acc, dv_far), (dk_acc, dk_far)):
                    added = acc[own, group_lanes(g)]
                    for h in members_of(g, heads):
                        added += masked(head_lanes(h), far[g, spot_of(h)])
                    acc[own, group_lanes(g)] = added

        dqt_ref[0, :, own] = (dq_acc[...] * scale).astype(BF16)

    dkrow_ref[0] = (dk_acc[...] * LN2).astype(BF16)
    dvrow_ref[0] = dv_acc[...].astype(BF16)


def feed_kernel(
    norm_ref, cot_ref, up_ref, down_ref, bias_ref, out_ref, back_ref, gup_ref, gdown_ref, gbias_ref,
    land, ret, parts, out_acc, back_acc, gup_acc, gdown_acc, gbias_acc, land_send, land_recv, ret_send,
    ret_recv, *, chunk, peers,
):
    v, j = pl.program_id(0), pl.program_id(1)
    steps = pl.num_programs(1)
    r = lax.axis_index("rows")

    def peer(k):
        to = r
        for bit in range(bits_of(peers)):
            if k >> bit & 1:
                to = flipped(to, bit)
        return {"rows": to}

    def landing(k):
        relayed = k % 2 == 1 and k > 1
        return pltpu.make_async_remote_copy(
            src_ref=land.at[k - 2] if relayed else norm_ref, dst_ref=land.at[k - 1],
            send_sem=land_send.at[k - 1], recv_sem=land_recv.at[k - 1],
            device_id=peer(1 if relayed else k),
        )

    def returning(k):
        return pltpu.make_async_remote_copy(
            src_ref=parts.at[k - 1], dst_ref=ret.at[k - 1], send_sem=ret_send.at[k - 1],
            recv_sem=ret_recv.at[k - 1], device_id=peer(k),
        )

    @pl.when((v == 0) & (j == 0))
    def _():
        barrier = pltpu.get_barrier_semaphore()
        for n in range(1, peers):
            pl.semaphore_signal(barrier, inc=1, device_id={"rows": (r + n) % peers})
        pl.semaphore_wait(barrier, peers - 1)
        for k in range(1, peers):
            if k == 1 or k % 2 == 0:
                landing(k).start()

    for k in range(1, peers):
        @pl.when((v == k - 1) & (j == 0))
        def _():
            landing(k).wait_recv()
            if k % 2 == 0 and k + 1 < peers:
                landing(k + 1).start()

        @pl.when((v == k) & (j == 1))
        def _():
            returning(k).start()

    here = pl.ds(pl.multiple_of(j * chunk, chunk), chunk)

    def work(norm):
        cot = cot_ref[0]
        up, down = up_ref[here, :], down_ref[here, :]
        pre = dot_nt(norm, up) + bias_ref[...]
        phi = 0.5 + 0.5 * lax.erf(pre * (1.0 / math.sqrt(2.0)))
        dens = jnp.exp(-0.5 * pre * pre) * (1.0 / math.sqrt(2.0 * math.pi))
        act = (pre * phi).astype(BF16)
        slope = dot_nt(cot, down) * (phi + pre * dens)
        slope_low = slope.astype(BF16)

        @pl.when(j == 0)
        def _():
            out_acc[...] = dot(act, down)
            back_acc[...] = dot(slope_low, up)

        @pl.when(j > 0)
        def _():
            out_acc[...] += dot(act, down)
            back_acc[...] += dot(slope_low, up)

        bias_sum = jnp.sum(slope_low.astype(F32), axis=0, keepdims=True)
        gup, gdown = dot_tn(slope_low, norm), dot_tn(act, cot)

        @pl.when(v == 0)
        def _():
            gup_acc[here, :] = gup
            gdown_acc[here, :] = gdown
            gbias_acc[pl.ds(j, 1)] = bias_sum

        @pl.when(v > 0)
        def _():
            gup_acc[here, :] += gup
            gdown_acc[here, :] += gdown
            gbias_acc[pl.ds(j, 1)] += bias_sum

    @pl.when(v < peers - 1)
    def _():
        work(land[jnp.minimum(v, peers - 2)])

    @pl.when(v == peers - 1)
    def _():
        work(norm_ref[...])

    @pl.when(j == steps - 1)
    def _():
        out_ref[0] = out_acc[...].astype(BF16)

    for k in range(1, peers):
        @pl.when((v == k - 1) & (j == steps - 1))
        def _():
            parts[k - 1] = back_acc[...].astype(BF16)

    @pl.when(v == peers - 1)
    def _():
        gup_ref[...] = gup_acc[here, :].astype(BF16)
        gdown_ref[...] = gdown_acc[here, :].astype(BF16)
        gbias_ref[0] = gbias_acc[pl.ds(j, 1)]

    @pl.when((v == peers - 1) & (j == steps - 1))
    def _():
        total = back_acc[...]
        for k in range(1, peers):
            returning(k).wait_recv()
            total += ret[k - 1].astype(F32)
        back_ref[...] = total
        for k in range(1, peers):
            landing(k).wait_send()
            returning(k).wait_send()


def reduce_kernel(parts_ref, vec_ref, sum_ref, all_ref, work, got, vwork, vgot, send, recv, vsend, vrecv, *, orders):
    rows, seq = lax.axis_size("rows"), lax.axis_size("seq")
    r, s = lax.axis_index("rows"), lax.axis_index("seq")
    barrier = pltpu.get_barrier_semaphore()
    count = len(orders[0])
    for axis, bit in orders[0]:
        pl.semaphore_signal(barrier, inc=1, device_id={axis: flipped(r if axis == "rows" else s, bit)})
    pl.semaphore_wait(barrier, count)

    total = parts_ref.shape[1]
    offset = [total - (total >> n) for n in range(count)]

    def current(color, n):
        return parts_ref.at[color] if n == 0 else work.at[color, pl.ds(offset[n - 1], total >> n)]

    def bit_of(color, n):
        axis, bit = orders[color][n]
        return bit_at(r if axis == "rows" else s, bit)

    def partner(color, n):
        axis, bit = orders[color][n]
        return {axis: flipped(r if axis == "rows" else s, bit)}

    def copy(color, n):
        half = total >> (n + 1)
        return pltpu.make_async_remote_copy(
            src_ref=current(color, n).at[pl.ds((1 - bit_of(color, n)) * half, half)],
            dst_ref=got.at[color, pl.ds(offset[n], half)],
            send_sem=send.at[color, n], recv_sem=recv.at[color, n], device_id=partner(color, n),
        )

    def vcopy(n):
        return pltpu.make_async_remote_copy(
            src_ref=vec_ref if n == 0 else vwork.at[n - 1], dst_ref=vgot.at[n],
            send_sem=vsend.at[n], recv_sem=vrecv.at[n], device_id=partner(0, n),
        )

    for color in range(2):
        copy(color, 0).start()
    vcopy(0).start()
    for n in range(count):
        half = total >> (n + 1)
        for color in range(2):
            copy(color, n).wait_recv()
            keep = current(color, n).at[pl.ds(bit_of(color, n) * half, half)]

            @pl.loop(0, half)
            def _(i):
                value = keep[i].astype(F32) + got[color, offset[n] + i].astype(F32)
                if n + 1 < count:
                    work[color, offset[n] + i] = value.astype(BF16)
                else:
                    sum_ref[color] = value

        vcopy(n).wait_recv()
        value = (vec_ref[...] if n == 0 else vwork[n - 1]) + vgot[n]
        if n + 1 < count:
            vwork[n] = value
            for color in range(2):
                copy(color, n + 1).start()
            vcopy(n + 1).start()
        else:
            all_ref[...] = value
    for n in range(count):
        for color in range(2):
            copy(color, n).wait_send()
        vcopy(n).wait_send()


def reduce_units(parts, vec, collective_id):
    rows, seq, unit, model = parts.shape
    orders = [list(reversed(order)) for order in gather_orders(rows, seq)]
    count, total = len(orders[0]), rows * seq
    parts = parts.reshape((2,) * count + (2, unit // 2, model))
    ordered = []
    for color, order in enumerate(orders):
        dims = []
        for axis, bit in order:
            top = bits_of(rows) if axis == "rows" else count
            dims.append(top - 1 - bit)
        half = lax.index_in_dim(parts, color, count, keepdims=False)
        ordered.append(half.transpose(dims + [count, count + 1]).reshape(total, unit // 2, model))
    flat = vec.reshape(-1, LANES)
    whole = lambda shape: pl.BlockSpec(memory_space=pltpu.VMEM)
    sems = pltpu.SemaphoreType.DMA
    sums, vec_sum = pl.pallas_call(
        partial(reduce_kernel, orders=orders),
        in_specs=[pl.BlockSpec(memory_space=pltpu.VMEM)] * 2,
        out_specs=[pl.BlockSpec(memory_space=pltpu.VMEM)] * 2,
        out_shape=[
            jax.ShapeDtypeStruct((2, unit // 2, model), F32), jax.ShapeDtypeStruct(flat.shape, F32)
        ],
        scratch_shapes=[
            pltpu.VMEM((2, total, unit // 2, model), BF16), pltpu.VMEM((2, total, unit // 2, model), BF16),
            pltpu.VMEM((count,) + flat.shape, F32), pltpu.VMEM((count,) + flat.shape, F32),
            sems((2, count)), sems((2, count)), sems((count,)), sems((count,)),
        ],
        compiler_params=pltpu.CompilerParams(
            collective_id=collective_id, has_side_effects=True, vmem_limit_bytes=VMEM_LIMIT
        ),
        name="reduce",
    )(jnp.stack(ordered), flat)
    return sums.reshape(unit, model), vec_sum.reshape(vec.shape)


def norm_stats(value):
    centre = jnp.mean(value, axis=-1, keepdims=True)
    centred = value - centre
    inverse = lax.rsqrt(jnp.mean(centred * centred, axis=-1, keepdims=True) + NORM_EPS)
    return centred * inverse, inverse


def norm_back(upstream, unit_rows, inverse, gain):
    scaled = upstream * gain
    centred_mean = jnp.mean(scaled, axis=-1, keepdims=True)
    along_unit = jnp.mean(scaled * unit_rows, axis=-1, keepdims=True)
    return inverse * (scaled - centred_mean - unit_rows * along_unit)


def on_device(
    tokens, segments, ln1_gain, ln1_bias, w_qkv, q_bias, v_bias, w_out, out_bias, ln2_gain,
    ln2_bias, w_up, up_bias, w_down, down_bias, cotangent,
):
    nrow, span, model = tokens.shape
    rows, seq = lax.axis_size("rows"), lax.axis_size("seq")
    count = nrow * span
    width = model // HEADS
    ri, si = lax.axis_index("rows"), lax.axis_index("seq")
    grad_scale = 1.0 / math.sqrt(rows * nrow * seq * span)
    params = partial(pltpu.CompilerParams, vmem_limit_bytes=VMEM_LIMIT)

    team = max(g for g in (1, 2, 4) if HEADS % g == 0 and seq % g == 0 and g * span <= SEG_MOST)
    chunks, chunk = seq // team, team * span
    halo = -(-(SEG_MOST - 1) // chunk)
    blocks = (2 * halo + 1) * team
    window = blocks * span
    heads = HEADS // team
    here = heads * width
    groups = -(-heads // GROUP)
    wide = groups * LANES
    member = si % team

    def fetch(value_for, dc, k):
        perm = []
        for c in range(chunks):
            for m in range(team):
                if 0 <= c + dc < chunks:
                    perm.append(((c + dc) * team + (m + k) % team, c * team + m))
        value = value_for((member - k) % team)
        if dc == 0 and k == 0:
            return value
        return lax.ppermute(value, "seq", perm)

    def fetch_window(value_for):
        got = [fetch(value_for, dc, k) for dc in range(-halo, halo + 1) for k in range(team)]
        return jnp.stack(got)

    def in_order(rotated, axis):
        if team == 1:
            return rotated[0]
        twice = jnp.concatenate(list(rotated) * 2, axis=axis)
        size = rotated[0].shape[axis]
        return lax.dynamic_slice_in_dim(twice, ((team - member) % team) * size, team * size, axis)

    unit = 4 * model // (rows * seq)
    qkv_units = 3 * rows // 4
    shards = jnp.concatenate([w_qkv, w_out], axis=1).reshape(model // rows, rows, unit)
    shards = exchange(shards.transpose(1, 2, 0), "rows")
    shards = shards.transpose(1, 0, 2).reshape(2, unit // 2, model)
    windows = partial(window_of, team=team, chunks=chunks, halo=halo)
    (tok_win, seg_win), units = windows([tokens[None], segments[None]], shards, 1, name="gather")
    qkv_t = units[:qkv_units].transpose(1, 0, 2, 3).reshape(3, team, here, model)
    out_t = units[qkv_units:].transpose(1, 0, 2, 3).reshape(model, model)
    at_chunk = si // team - halo + jnp.arange(blocks, dtype=jnp.int32) // team
    inside = (at_chunk >= 0) & (at_chunk < chunks)
    segs = jnp.where(inside[:, None, None], seg_win, -1) + 1
    segs = segs.transpose(1, 0, 2).reshape(nrow, window)
    tok_win, w_up, w_down, late_cotangent = lax.optimization_barrier(
        (tok_win, w_up, w_down, cotangent)
    )

    ff = up_bias.shape[0]
    hid = ff // rows
    part = ff // (rows * seq)
    both = jnp.stack([w_up.T, w_down])
    both = both.reshape(2, rows, part, model // rows)
    mine = exchange(both.transpose(1, 0, 2, 3), "rows")
    mine = mine.transpose(1, 2, 0, 3).reshape(2, part, model)
    feed_w = lax.all_gather(mine, "seq", axis=1, tiled=False).reshape(2, hid, model)
    my_up_bias = lax.dynamic_index_in_dim(
        up_bias.astype(F32).reshape(seq, rows, part), ri, 1, keepdims=False
    ).reshape(1, hid)

    cot_low = cotangent.reshape(count, model)
    late_cot = late_cotangent.reshape(count, model)
    cot_all = jnp.stack([swap(late_cot, "rows", k) if k else late_cot for k in range(rows)])

    gain_one, gain_two = ln1_gain.astype(F32)[None], ln2_gain.astype(F32)[None]
    shift_one, shift_two = ln1_bias.astype(F32)[None], ln2_bias.astype(F32)[None]
    my_w = lax.dynamic_index_in_dim(qkv_t, member, 1, keepdims=False)
    qb = lax.dynamic_index_in_dim(q_bias.astype(F32).reshape(team, here), member, 0, keepdims=False)
    vb = lax.dynamic_index_in_dim(v_bias.astype(F32).reshape(team, here), member, 0, keepdims=False)
    pad_w = [pad_heads(my_w[i], 0, heads) for i in range(3)]
    pad_qb, pad_vb = pad_heads(qb, 0, heads), pad_heads(vb, 0, heads)
    w_row = jnp.concatenate(pad_w, axis=0)
    b_row = jnp.concatenate([pad_qb, jnp.zeros_like(pad_qb), pad_vb])[None]
    w_col = jnp.concatenate([pad_w[0], my_w[1], my_w[2]], axis=0)
    b_col = jnp.concatenate([pad_qb, jnp.zeros_like(qb), vb])[:, None]

    whole = lambda *shape: pl.BlockSpec(shape, lambda *_: (0,) * len(shape))
    row_spec = pl.BlockSpec((1, span, wide), lambda r, b: (r, b, 0))
    col_spec = lambda size: pl.BlockSpec((1, size, span), lambda r, b: (r, 0, b))
    row_shape = jax.ShapeDtypeStruct((nrow, window, wide), BF16)
    col_shape = lambda size: jax.ShapeDtypeStruct((nrow, size, window), BF16)
    krow, vrow, qrow, kt, vt, qt = pl.pallas_call(
        partial(qkv_kernel, scale=LOG2E / math.sqrt(width)),
        grid_spec=pltpu.PrefetchScalarGridSpec(
            num_scalar_prefetch=0,
            grid=(nrow, blocks),
            in_specs=[
                pl.BlockSpec((1, 1, span, model), lambda r, b: (b, r, 0, 0)),
                pl.BlockSpec((1, span, 1), lambda r, b: (r, b, 0)),
                pl.BlockSpec((1, 1, span), lambda r, b: (r, 0, b)),
                whole(1, model), whole(1, model), whole(3 * wide, model), whole(1, 3 * wide),
                whole(wide + 2 * here, model), whole(wide + 2 * here, 1),
            ],
            out_specs=[row_spec] * 3 + [col_spec(here), col_spec(here), col_spec(wide)],
        ),
        out_shape=[row_shape] * 3 + [col_shape(here), col_shape(here), col_shape(wide)],
        compiler_params=params(),
        name="qkv",
    )(tok_win, segs[:, :, None], segs[:, None, :], gain_one, shift_one, w_row, b_row, w_col, b_col)

    tiles, start = chunk // TILE, halo * chunk // TILE
    own_segs = lax.slice_in_dim(segs, halo * chunk, (halo + 1) * chunk, axis=1)
    own_segs = own_segs.reshape(nrow, tiles, TILE)
    at = jnp.arange(window, dtype=jnp.int32)
    first = jnp.min(
        jnp.where(segs[:, None, :] == own_segs[:, :, :1], at, window), axis=-1
    ) // TILE
    last = jnp.max(jnp.where(segs[:, None, :] == own_segs[:, :, -1:], at, 0), axis=-1) // TILE

    once = pl.Buffered(1)
    per_row = lambda *shape: pl.BlockSpec(
        (1,) + shape, lambda r, *_: (r,) + (0,) * len(shape), pipeline_mode=once
    )
    stat = -(-heads // 8) * 8
    attended_t, lse = pl.pallas_call(
        partial(attend_kernel, heads=heads),
        grid_spec=pltpu.PrefetchScalarGridSpec(
            num_scalar_prefetch=2,
            grid=(nrow,),
            in_specs=[
                per_row(window, wide), per_row(here, window),
                pl.BlockSpec((1, wide, chunk), lambda r, *_: (r, 0, halo), pipeline_mode=once),
            ],
            out_specs=[per_row(here, chunk), per_row(stat, chunk)],
            scratch_shapes=[
                pltpu.VMEM((groups, LANES, GROUP * TILE), BF16),
                pltpu.VMEM((8, GROUP * TILE), F32), pltpu.VMEM((8, GROUP * TILE), F32),
                pltpu.VMEM((here, TILE), F32),
            ],
        ),
        out_shape=[
            jax.ShapeDtypeStruct((nrow, here, chunk), BF16),
            jax.ShapeDtypeStruct((nrow, stat, chunk), F32),
        ],
        compiler_params=params(),
        name="attend",
    )(first, last, krow, vt, qt)

    by_member = attended_t.reshape(nrow, here, team, span)
    joined = in_order(
        [
            fetch(lambda m: lax.dynamic_index_in_dim(by_member, m, 2, keepdims=False), 0, k)
            for k in range(team)
        ],
        1,
    )
    attended = joined.transpose(0, 2, 1).reshape(count, model)
    lse_parts = []
    for dc in range(-halo, halo + 1):
        if dc == 0:
            lse_parts.append(lse)
        else:
            perm = [
                ((c + dc) * team + m, c * team + m)
                for c in range(chunks) for m in range(team) if 0 <= c + dc < chunks
            ]
            lse_parts.append(lax.ppermute(lse, "seq", perm))
    lse_window = jnp.concatenate(lse_parts, axis=2)

    flat_tokens = tokens.reshape(count, model).astype(F32)
    residual = flat_tokens + dot_nt(attended, out_t) + out_bias.astype(F32)
    unit_two, inverse_two = norm_stats(residual)
    normed_two = (unit_two * gain_two + shift_two).astype(BF16)

    step = 256 if hid % 256 == 0 else LANES
    once = pl.Buffered(1)
    order_spec = pl.BlockSpec((1, count, model), lambda v, j: ((v + 1) % rows, 0, 0))
    whole_once = lambda *shape: pl.BlockSpec(shape, lambda *_: (0,) * len(shape), pipeline_mode=once)
    grad_spec = pl.BlockSpec((step, model), lambda v, j: (jnp.where(v == rows - 1, j, 0), 0))
    sems = pltpu.SemaphoreType.DMA
    block = pltpu.VMEM((rows - 1, count, model), BF16)
    out_parts, normed_two_grad, grad_up, grad_down, grad_up_bias = pl.pallas_call(
        partial(feed_kernel, chunk=step, peers=rows),
        grid=(rows, hid // step),
        in_specs=[
            whole_once(count, model), order_spec, whole_once(hid, model), whole_once(hid, model),
            pl.BlockSpec((1, step), lambda v, j: (0, j)),
        ],
        out_specs=[
            order_spec, whole_once(count, model), grad_spec, grad_spec,
            pl.BlockSpec((1, 1, step), lambda v, j: (jnp.where(v == rows - 1, j, 0), 0, 0)),
        ],
        out_shape=[
            jax.ShapeDtypeStruct((rows, count, model), BF16),
            jax.ShapeDtypeStruct((count, model), F32),
            jax.ShapeDtypeStruct((hid, model), BF16),
            jax.ShapeDtypeStruct((hid, model), BF16),
            jax.ShapeDtypeStruct((hid // step, 1, step), F32),
        ],
        scratch_shapes=[
            block, block, block,
            pltpu.VMEM((count, model), F32), pltpu.VMEM((count, model), F32),
            pltpu.VMEM((hid, model), F32), pltpu.VMEM((hid, model), F32),
            pltpu.VMEM((hid // step, step), F32),
            *[sems((rows - 1,))] * 4,
        ],
        compiler_params=params(collective_id=4, has_side_effects=True),
        name="feed",
    )(normed_two, cot_all, feed_w[0], feed_w[1], my_up_bias)

    result = residual + down_bias.astype(F32) + out_parts[0].astype(F32)
    for k in range(1, rows):
        result = result + swap(out_parts[k], "rows", k).astype(F32)
    output = result.astype(BF16).reshape(tokens.shape)

    feed_grad = jnp.stack(
        [grad_up.reshape(seq, part, model), grad_down.reshape(seq, part, model)], axis=1
    )
    feed_sum = lax.psum_scatter(feed_grad, "seq", scatter_dimension=0, tiled=False)
    feed_sum = feed_sum.reshape(2, part, rows, model // rows)
    back = exchange(feed_sum.transpose(2, 0, 1, 3), "rows")
    back = back.transpose(1, 0, 2, 3).reshape(2, ff // seq, model // rows).astype(F32) * grad_scale
    sum_up, sum_down = back[0].T, back[1]

    cot_wide = cot_low.astype(F32)
    grad_gain_two = jnp.sum(normed_two_grad * unit_two, axis=0)
    grad_shift_two = jnp.sum(normed_two_grad, axis=0)
    residual_grad = cot_wide + norm_back(normed_two_grad, unit_two, inverse_two, gain_two)
    branch_grad = residual_grad.astype(BF16)
    grad_out_t = dot_tn(branch_grad, attended).astype(BF16)
    grad_out_bias = jnp.sum(branch_grad, axis=0, dtype=F32)
    attended_grad = dot(branch_grad, out_t).astype(BF16)

    wide_bias = jnp.zeros((seq, rows, part), F32)
    wide_bias = lax.dynamic_update_index_in_dim(
        wide_bias, grad_up_bias.reshape(seq, part), ri, 1
    ).reshape(ff)
    early = [
        grad_out_bias, grad_gain_two, grad_shift_two, jnp.sum(cot_low, axis=0, dtype=F32), wide_bias,
    ]

    delta = jnp.sum(
        (attended.astype(F32) * attended_grad.astype(F32)).reshape(nrow, span, HEADS, width), axis=-1
    ).transpose(0, 2, 1)
    delta = jnp.pad(delta.reshape(nrow, team, heads, span), ((0, 0), (0, 0), (0, stat - heads), (0, 0)))
    grad_members = attended_grad.reshape(nrow, span, team, here)
    grad_win, delta_win = windows(
        [grad_members.transpose(2, 0, 1, 3), delta.transpose(1, 0, 2, 3)], None, 2, name="grads"
    )
    grad_win = grad_win.transpose(1, 0, 2, 3).reshape(nrow, window, here)
    delta_win = delta_win.transpose(1, 2, 0, 3).reshape(nrow, stat, window)
    grow = pad_heads(grad_win, 2, heads)
    gt = grow.transpose(0, 2, 1)

    dqt, dkrow, dvrow = pl.pallas_call(
        partial(back_kernel, heads=heads, start=start),
        grid_spec=pltpu.PrefetchScalarGridSpec(
            num_scalar_prefetch=2,
            grid=(nrow,),
            in_specs=[
                per_row(window, wide), per_row(window, wide), per_row(window, wide),
                per_row(here, window), per_row(wide, window), per_row(window, wide),
                per_row(wide, window), per_row(stat, window), per_row(stat, window),
            ],
            out_specs=[per_row(here, chunk), per_row(chunk, wide), per_row(chunk, wide)],
            scratch_shapes=[
                *[pltpu.VMEM((groups, LANES, GROUP * TILE), BF16)] * 2,
                *[pltpu.VMEM((groups, GROUP * TILE, LANES), BF16)] * 4,
                pltpu.VMEM((2, 8, GROUP * TILE), F32),
                pltpu.VMEM((chunk, wide), F32), pltpu.VMEM((chunk, wide), F32),
                pltpu.VMEM((here, TILE), F32),
                *[pltpu.VMEM((groups, GROUP * TILE, LANES), F32)] * 2,
            ],
        ),
        out_shape=[
            jax.ShapeDtypeStruct((nrow, here, chunk), BF16),
            jax.ShapeDtypeStruct((nrow, chunk, wide), BF16),
            jax.ShapeDtypeStruct((nrow, chunk, wide), BF16),
        ],
        compiler_params=params(),
        name="attend_back",
    )(first, last, krow, vrow, qrow, kt, qt, grow, gt, lse_window, delta_win)

    mixed = jnp.concatenate(
        [dqt.transpose(0, 2, 1), drop_pad(dkrow, 2, heads, width), drop_pad(dvrow, 2, heads, width)],
        axis=2,
    )
    mixed_flat = mixed.reshape(nrow * chunk, 3 * here)
    chunk_tokens = tok_win[halo * team : (halo + 1) * team].transpose(1, 0, 2, 3)
    chunk_unit, _ = norm_stats(chunk_tokens.astype(F32).reshape(nrow * chunk, model))
    chunk_norm = (chunk_unit * gain_one + shift_one).astype(BF16)
    grad_qkv_t = dot_tn(mixed_flat, chunk_norm).astype(BF16)
    bias_sums = jnp.sum(mixed_flat, axis=0, dtype=F32).reshape(3, here)
    back_part = dot(mixed_flat, my_w.reshape(3 * here, model)).astype(BF16)
    back_members = back_part.reshape(nrow, team, span, model)
    normed_one_grad = 0.0
    for k in range(team):
        normed_one_grad = normed_one_grad + fetch(
            lambda m: lax.dynamic_index_in_dim(back_members, m, 1, keepdims=False), 0, k
        ).astype(F32)
    normed_one_grad = normed_one_grad.reshape(count, model)
    unit_one, inverse_one = norm_stats(flat_tokens)
    grad_gain_one = jnp.sum(normed_one_grad * unit_one, axis=0)
    grad_shift_one = jnp.sum(normed_one_grad, axis=0)
    tokens_grad = residual_grad + norm_back(normed_one_grad, unit_one, inverse_one, gain_one)
    tokens_grad = tokens_grad.astype(BF16).reshape(tokens.shape)

    at_member = (jnp.arange(team) == member)[None, :, None, None]
    spread = jnp.where(at_member, grad_qkv_t.reshape(3, 1, here, model), jnp.zeros((), BF16))
    spread = spread.reshape(seq, qkv_units, unit, model)
    spread = jnp.concatenate([spread, grad_out_t.reshape(seq, rows - qkv_units, unit, model)], axis=1)
    bias_full = jnp.where(at_member[:, :, 0], bias_sums[0::2][:, None], 0.0)
    flat = jnp.concatenate([*early, grad_gain_one, grad_shift_one, bias_full.reshape(2 * model)])
    sums, flat = reduce_units(spread.transpose(1, 0, 2, 3), flat, 3)
    flat = flat * grad_scale
    sums = exchange(sums.reshape(unit, rows, model // rows).transpose(1, 0, 2), "rows")
    sums = sums.reshape(rows * unit, model // rows).T.astype(F32) * grad_scale
    sum_qkv, sum_out = sums[:, : qkv_units * unit], sums[:, qkv_units * unit :]

    sum_out_bias, sum_gain_two, sum_shift_two, sum_down_bias = (
        flat[i * model : (i + 1) * model] for i in range(4)
    )
    sum_up_bias = flat[4 * model : 4 * model + ff]
    sum_gain_one, sum_shift_one, sum_q_bias, sum_v_bias = (
        flat[4 * model + ff + i * model : 4 * model + ff + (i + 1) * model] for i in range(4)
    )

    return (
        output, tokens_grad, sum_gain_one, sum_shift_one, sum_qkv, sum_q_bias, sum_v_bias, sum_out,
        sum_out_bias, sum_gain_two, sum_shift_two, sum_up, sum_up_bias, sum_down, sum_down_bias,
    )


def solution(mesh):
    tok, mat, rep = P("rows", "seq", None), P("rows", "seq"), P()
    in_specs = (
        tok, mat, rep, rep, mat, rep, rep, mat, rep, rep, rep, mat, rep, P("seq", "rows"), rep, tok,
    )
    out_specs = (
        tok, tok, rep, rep, mat, rep, rep, mat, rep, rep, rep, mat, rep, P("seq", "rows"), rep,
    )
    return jax.shard_map(
        on_device, mesh=mesh, in_specs=in_specs, out_specs=out_specs, check_vma=False
    )
```
